32 devices in a mesh: dp: 4 (over z), row: 4 (over y, core), col: 2 (over x).
Axes of the slice: x: 2, y: 2, z: 4, core: 2. Of those that a mesh axis runs over, the one named last changes fastest.
Arguments:
- x_in: bfloat16 [2048, 1024], P(('dp', 'col'), 'row'), may hold values from -30 to 30
- norm_gain: float32 [1024], P('row'), may hold values from 0.1 to 1.9
- b_weight: bfloat16 [1024, 1024], P('row', 'col'), may hold values from -0.1875 to 0.1875
- c_weight: bfloat16 [1024, 1024], P('row', 'col'), may hold values from -0.1875 to 0.1875
- x_weight: bfloat16 [1024, 1024], P('row', 'col'), may hold values from -0.1875 to 0.1875
- conv_weight: float32 [3, 1024], P(None, 'col'), may hold values from -3 to 3
- out_weight: bfloat16 [1024, 1024], P('col', 'row'), may hold values from -0.1875 to 0.1875
- ffn_gain: float32 [1024], P('row'), may hold values from 0.1 to 1.9
- gate_weight: bfloat16 [1024, 4608], P('row', 'col'), may hold values from -0.1875 to 0.1875
- up_weight: bfloat16 [1024, 4608], P('row', 'col'), may hold values from -0.1875 to 0.1875
- down_weight: bfloat16 [4608, 1024], P('col', 'row'), may hold values from -0.1875 to 0.1875
- cotangent: bfloat16 [2048, 1024], P(('dp', 'col'), 'row'), may hold values from -16 to 16
Outputs:
- block_out: float32 [2048, 1024], P(('dp', 'col'), 'row')
- x_grad: float32 [2048, 1024], P(('dp', 'col'), 'row')
- norm_gain_grad: float32 [1024], P('row')
- b_weight_grad: float32 [1024, 1024], P('row', 'col')
- c_weight_grad: float32 [1024, 1024], P('row', 'col')
- x_weight_grad: float32 [1024, 1024], P('row', 'col')
- conv_weight_grad: float32 [3, 1024], P(None, 'col')
- out_weight_grad: float32 [1024, 1024], P('col', 'row')
- ffn_gain_grad: float32 [1024], P('row')
- gate_weight_grad: float32 [1024, 4608], P('row', 'col')
- up_weight_grad: float32 [1024, 4608], P('row', 'col')
- down_weight_grad: float32 [4608, 1024], P('col', 'row')
The draws below stay inside these ranges and needn't reach their ends.
All inputs are finite; a program needn't handle non-finite values.
Results may differ from the reference program's by a relative error of at most 0.0081.
Values may be sent and summed in bfloat16 or wider, within the bound.
No kernel may reach another device: no remote copies, remote signals or barrier semaphores. Data moves between devices by JAX's collectives and lax.ppermute only.
A program may use at most 128 MiB of HBM per device.

```python
import jax
import jax.numpy as jnp
from jax import lax

D = 1024
FF = 4608
LEN = 128
TOKENS = 2048
N_DP = 4


def draw_x_in(key, part):
    first_key, second_key = jax.random.split(key)
    column_scale = 0.3 * 10.0 ** (jnp.arange(D, dtype=jnp.float32) / D)
    row_scale = 10.0 ** jax.random.uniform(second_key, (TOKENS, 1), jnp.float32, -0.3, 0.3)
    values = jnp.clip(jax.random.normal(first_key, (TOKENS, D), jnp.float32), -5.0, 5.0)
    return (values * column_scale[None, :] * row_scale).astype(jnp.bfloat16)


def draw_cotangent(key, part):
    first_key, second_key = jax.random.split(key, 2)
    position = jnp.arange(TOKENS, dtype=jnp.float32) / TOKENS
    row_scale = 0.6 * 3.0 ** position * 10.0 ** jax.random.uniform(second_key, (TOKENS,), jnp.float32, -0.2, 0.2)
    values = jnp.clip(jax.random.normal(first_key, (TOKENS, D), jnp.float32), -5.0, 5.0)
    return (values * row_scale[:, None]).astype(jnp.bfloat16)


def shard_levels(stream_key, extent, pieces, low, largest):
    factor_of = 1.0
    for axis_at, parts in pieces:
        heights = jax.random.uniform(jax.random.fold_in(jax.random.fold_in(stream_key, 6), axis_at), (parts,), jnp.float32, low / len(pieces), largest / len(pieces))
        factor_of = factor_of * jnp.repeat(jnp.exp(heights), extent[axis_at] // parts).reshape((-1,) + (1,) * (len(extent) - 1 - axis_at))
    return factor_of


def noise(stream_key, shape, width, reach, cuts=(), held_as=jnp.bfloat16):
    loudness = shard_levels(stream_key, shape, cuts, -0.22, 0.18) if cuts else 1.0
    values = jax.random.normal(stream_key, shape, jnp.float32) * width * loudness
    return jnp.minimum(jnp.maximum(values, -reach), reach).astype(held_as)


def setup_inputs(seed: int = 0) -> dict:
    streams_of = jax.random.split(jax.random.key(seed), 13)
    x_in = draw_x_in(jax.random.fold_in(streams_of[12], 71), 0)
    norm_gain = jnp.clip(1.0 + 0.18 * jax.random.normal(streams_of[1], (D,), jnp.float32), 0.1, 1.9)
    b_weight = noise(streams_of[2], (D, D), D ** -0.5, 0.1875, ((0, 4), (1, 2)))
    c_weight = noise(streams_of[3], (D, D), D ** -0.5, 0.1875, ((0, 4), (1, 2)))
    x_weight = noise(streams_of[4], (D, D), D ** -0.5, 0.1875, ((0, 4), (1, 2)))
    conv_weight = noise(streams_of[5], (3, D), 0.6, 3.0, ((1, 2),), jnp.float32)
    out_weight = noise(streams_of[6], (D, D), D ** -0.5, 0.1875, ((0, 2), (1, 4)))
    ffn_gain = jnp.clip(1.0 + 0.18 * jax.random.normal(streams_of[7], (D,), jnp.float32), 0.1, 1.9)
    gate_weight = noise(streams_of[8], (D, FF), D ** -0.5, 0.1875, ((0, 4), (1, 2)))
    up_weight = noise(streams_of[9], (D, FF), D ** -0.5, 0.1875, ((0, 4), (1, 2)))
    down_weight = noise(streams_of[10], (FF, D), (FF // 4) ** -0.5, 0.1875, ((0, 2), (1, 4)))
    cotangent = draw_cotangent(jax.random.fold_in(streams_of[12], 71), 0)
    return {"x_in": x_in, "norm_gain": norm_gain, "b_weight": b_weight, "c_weight": c_weight, "x_weight": x_weight, "conv_weight": conv_weight, "out_weight": out_weight, "ffn_gain": ffn_gain, "gate_weight": gate_weight, "up_weight": up_weight, "down_weight": down_weight, "cotangent": cotangent}


EPSILON = 1e-05

def contract_rows(left_side, right_side):
    return lax.dot_general(left_side, right_side, (((0,), (0,)), ((), ())), preferred_element_type=jnp.float32)

def against(left_side, right_side):
    return lax.dot_general(left_side, right_side, (((1,), (1,)), ((), ())), preferred_element_type=jnp.float32)

def causal_conv(values, kernel):
    channels = values.shape[1]
    padded = jnp.pad(values.reshape(-1, LEN, channels), ((0, 0), (2, 0), (0, 0)))
    result = kernel[0] * padded[:, :-2] + kernel[1] * padded[:, 1:-1] + kernel[2] * padded[:, 2:]
    return result.reshape(values.shape)

def conv_backward(mixed_rows, conv_delta, kernel):
    channels = mixed_rows.shape[1]
    mixed_seqs = jnp.pad(mixed_rows.reshape(-1, LEN, channels), ((0, 0), (2, 0), (0, 0)))
    delta_seqs = conv_delta.reshape(-1, LEN, channels)
    kernel_grad = jnp.stack([lax.optimization_barrier(jnp.sum(delta_seqs * mixed_seqs[:, :-2], axis=(0, 1))), lax.optimization_barrier(jnp.sum(delta_seqs * mixed_seqs[:, 1:-1], axis=(0, 1))), lax.optimization_barrier(jnp.sum(delta_seqs * mixed_seqs[:, 2:], axis=(0, 1)))])
    delta_padded = jnp.pad(delta_seqs, ((0, 0), (0, 2), (0, 0)))
    mixed_delta = kernel[0] * delta_padded[:, 2:] + kernel[1] * delta_padded[:, 1:-1] + kernel[2] * delta_padded[:, :-2]
    return (kernel_grad, mixed_delta.reshape(mixed_rows.shape))

def norm_backward(upstream, values, inverse, gain_vector):
    scaled = upstream * gain_vector[None, :]
    average = lax.optimization_barrier(jnp.mean(scaled * values, axis=1))
    return inverse[:, None] * scaled - values * (inverse * inverse * inverse * average)[:, None]

def one_block(x_in, norm_gain, b_weight, c_weight, x_weight, conv_weight, out_weight, ffn_gain, gate_weight, up_weight, down_weight, cotangent):
    inputs = x_in.astype(jnp.float32)
    inv_first = lax.rsqrt(lax.optimization_barrier(jnp.mean(inputs * inputs, axis=1)) + EPSILON)
    normed_one = (inputs * inv_first[:, None] * norm_gain[None, :]).astype(jnp.bfloat16)
    b_sum = jnp.dot(normed_one, b_weight, preferred_element_type=jnp.float32)
    c_sum = jnp.dot(normed_one, c_weight, preferred_element_type=jnp.float32)
    x_sum = jnp.dot(normed_one, x_weight, preferred_element_type=jnp.float32)
    mixed_rows = b_sum * x_sum
    conv_out = causal_conv(mixed_rows, conv_weight)
    gated_mix = (c_sum * conv_out).astype(jnp.bfloat16)
    hidden = inputs + jnp.dot(gated_mix, out_weight, preferred_element_type=jnp.float32)
    inv_second = lax.rsqrt(lax.optimization_barrier(jnp.mean(hidden * hidden, axis=1)) + EPSILON)
    normed_two = (hidden * inv_second[:, None] * ffn_gain[None, :]).astype(jnp.bfloat16)
    gate_sum = jnp.dot(normed_two, gate_weight, preferred_element_type=jnp.float32)
    up_sum = jnp.dot(normed_two, up_weight, preferred_element_type=jnp.float32)
    sigmoid_gate = jax.nn.sigmoid(gate_sum)
    activation = (gate_sum * sigmoid_gate * up_sum).astype(jnp.bfloat16)
    block_out = hidden + jnp.dot(activation, down_weight, preferred_element_type=jnp.float32)
    down_grad = contract_rows(activation, cotangent)
    act_delta = against(cotangent, down_weight)
    gate_delta = (act_delta * up_sum * sigmoid_gate * (1.0 + gate_sum * (1.0 - sigmoid_gate))).astype(jnp.bfloat16)
    up_delta = (act_delta * gate_sum * sigmoid_gate).astype(jnp.bfloat16)
    gate_grad = contract_rows(normed_two, gate_delta)
    up_grad = contract_rows(normed_two, up_delta)
    normed_two_delta = against(gate_delta, gate_weight) + against(up_delta, up_weight)
    ffn_gain_grad = lax.optimization_barrier(jnp.sum(normed_two_delta * hidden * inv_second[:, None], axis=0))
    hidden_delta = cotangent.astype(jnp.float32) + norm_backward(normed_two_delta, hidden, inv_second, ffn_gain)
    mix_delta = hidden_delta.astype(jnp.bfloat16)
    out_grad = contract_rows(gated_mix, mix_delta)
    gated_delta = against(mix_delta, out_weight)
    c_delta = (gated_delta * conv_out).astype(jnp.bfloat16)
    conv_delta = gated_delta * c_sum
    conv_grad, mixed_delta = conv_backward(mixed_rows, conv_delta, conv_weight)
    b_delta = (mixed_delta * x_sum).astype(jnp.bfloat16)
    x_delta = (mixed_delta * b_sum).astype(jnp.bfloat16)
    b_grad = contract_rows(normed_one, b_delta)
    c_grad = contract_rows(normed_one, c_delta)
    x_weight_grad = contract_rows(normed_one, x_delta)
    normed_one_delta = against(b_delta, b_weight) + against(c_delta, c_weight) + against(x_delta, x_weight)
    norm_gain_grad = lax.optimization_barrier(jnp.sum(normed_one_delta * inputs * inv_first[:, None], axis=0))
    x_grad = hidden_delta + norm_backward(normed_one_delta, inputs, inv_first, norm_gain)
    gradients = (norm_gain_grad, b_grad, c_grad, x_weight_grad, conv_grad, out_grad, ffn_gain_grad, gate_grad, up_grad, down_grad)
    return ((block_out, x_grad), gradients)

def reference(x_in, norm_gain, b_weight, c_weight, x_weight, conv_weight, out_weight, ffn_gain, gate_weight, up_weight, down_weight, cotangent):
    group_rows = x_in.shape[0] // N_DP
    blocks_in = x_in.reshape(N_DP, group_rows, x_in.shape[1])
    blocks_cot = cotangent.reshape(N_DP, group_rows, cotangent.shape[1])
    shapes = (norm_gain, b_weight, c_weight, x_weight, conv_weight, out_weight, ffn_gain, gate_weight, up_weight, down_weight)
    initial = tuple((jnp.zeros(array.shape, jnp.float32) for array in shapes))

    def scan_step(carried, blocks):
        outputs, gradients = one_block(blocks[0], norm_gain, b_weight, c_weight, x_weight, conv_weight, out_weight, ffn_gain, gate_weight, up_weight, down_weight, blocks[1])
        return (tuple((total + part_sum for total, part_sum in zip(carried, gradients))), outputs)
    sums, outputs = lax.scan(scan_step, initial, (blocks_in, blocks_cot))
    block_out = outputs[0].reshape(x_in.shape)
    x_grad = outputs[1].reshape(x_in.shape)
    return (block_out, x_grad, sums[0], sums[1], sums[2], sums[3], sums[4], sums[5], sums[6], sums[7], sums[8], sums[9])
```

```python
import jax
import jax.numpy as jnp
from jax import lax
from jax.sharding import PartitionSpec as P

LEN = 128
EPSILON = 1e-05
BF = jnp.bfloat16
F32 = jnp.float32
EXTRA = 8


def dot_rows(left_side, right_side):
    return lax.dot_general(
        left_side, right_side, (((0,), (0,)), ((), ())), preferred_element_type=F32
    )


def dot_against(left_side, right_side):
    return lax.dot_general(
        left_side, right_side, (((1,), (1,)), ((), ())), preferred_element_type=F32
    )


def dot_plain(left_side, right_side):
    return jnp.dot(left_side, right_side, preferred_element_type=F32)


def pick(values, index, axis=0):
    return lax.dynamic_index_in_dim(values, index, axis, keepdims=False)


def causal_conv(values, kernel):
    channels = values.shape[1]
    padded = jnp.pad(values.reshape(-1, LEN, channels), ((0, 0), (2, 0), (0, 0)))
    result = kernel[0] * padded[:, :-2] + kernel[1] * padded[:, 1:-1] + kernel[2] * padded[:, 2:]
    return result.reshape(values.shape)


def conv_backward(mixed_rows, conv_delta, kernel):
    channels = mixed_rows.shape[1]
    mixed_seqs = jnp.pad(mixed_rows.reshape(-1, LEN, channels), ((0, 0), (2, 0), (0, 0)))
    delta_seqs = conv_delta.reshape(-1, LEN, channels)
    kernel_grad = jnp.stack(
        [
            jnp.sum(delta_seqs * mixed_seqs[:, :-2], axis=(0, 1)),
            jnp.sum(delta_seqs * mixed_seqs[:, 1:-1], axis=(0, 1)),
            jnp.sum(delta_seqs * mixed_seqs[:, 2:], axis=(0, 1)),
        ]
    )
    delta_padded = jnp.pad(delta_seqs, ((0, 0), (0, 2), (0, 0)))
    mixed_delta = (
        kernel[0] * delta_padded[:, 2:]
        + kernel[1] * delta_padded[:, 1:-1]
        + kernel[2] * delta_padded[:, :-2]
    )
    return kernel_grad, mixed_delta.reshape(mixed_rows.shape)


def solution(mesh):
    Z, R, C = mesh.shape["dp"], mesh.shape["row"], mesh.shape["col"]

    def swap_row(values, k):
        if k == 0:
            return values
        return lax.ppermute(values, "row", [(i, i ^ k) for i in range(R)])

    def swap_dp(values, k):
        if k == 0:
            return values
        return lax.ppermute(values, "dp", [(i, i ^ k) for i in range(Z)])

    def swap_plane(values, key):
        kr, kc = key
        moves = [
            (i * C + j, (i ^ kr) * C + (j ^ kc)) for i in range(R) for j in range(C)
        ]
        return lax.ppermute(values, ("row", "col"), moves)

    high = [(kr, 0) for kr in range(2, R, 2)]
    wide = [(0, kc) for kc in range(1, C)]
    core = [(1, 0)]
    staged = [high, wide, core]
    if (R // 2) * C <= 4:
        direct = [[(kr, kc) for kr in range(0, R, 2) for kc in range(C)][1:], core]
    else:
        direct = staged
    keys = [(kr, kc) for kr in range(R) for kc in range(C)]

    def xor(a, b):
        return (a[0] ^ b[0], a[1] ^ b[1])

    def gather(piece, stages):
        held = {(0, 0): piece}
        for stage in stages:
            names = list(held)
            payload = jnp.stack([held[n] for n in names]) if len(names) > 1 else held[names[0]][None]
            for offset in stage:
                got = swap_plane(payload, offset)
                for at, name in enumerate(names):
                    held[xor(name, offset)] = got[at]
        return held

    def scatter_sum(pieces, stages):
        for at in range(len(stages) - 1, -1, -1):
            after = [(0, 0)]
            for stage in stages[:at]:
                after = after + [xor(n, o) for o in stage for n in after]
            total = {n: pieces[n] for n in after}
            for offset in stages[at]:
                payload = jnp.stack([pieces[xor(n, offset)].astype(BF) for n in after])
                got = swap_plane(payload, offset)
                for i, n in enumerate(after):
                    total[n] = total[n] + got[i].astype(F32)
            pieces = total
        return pieces[(0, 0)]

    def local(
        x_in,
        norm_gain,
        b_weight,
        c_weight,
        x_weight,
        conv_weight,
        out_weight,
        ffn_gain,
        gate_weight,
        up_weight,
        down_weight,
        cotangent,
    ):
        z = lax.axis_index("dp")
        r = lax.axis_index("row")
        TB, FB = x_in.shape
        D = FB * R
        TP = TB // R
        MW = b_weight.shape[1] // R
        FW = gate_weight.shape[1] // R

        gains = jnp.stack([norm_gain, ffn_gain])
        part_a = lax.reduce_precision(gains, 8, 7)
        part_b = lax.reduce_precision(gains - part_a, 8, 7)
        part_c = gains - part_a - part_b
        gain_rows = jnp.concatenate([part_a, part_b, part_c]).astype(BF)
        gain_rows = jnp.pad(gain_rows, ((0, 16 - gain_rows.shape[0]), (0, 0)))
        blocks = gather(jnp.concatenate([x_in, gain_rows]), direct)
        by_row = jnp.stack([jnp.stack([blocks[(kr, kc)] for kc in range(C)]) for kr in range(R)])
        joined = jnp.concatenate([pick(by_row, r ^ b) for b in range(R)], axis=-1)
        x_rows = joined[:, :TB].reshape(C * TB, D)
        gain_all = joined[0, TB : TB + 6].astype(F32)
        gain_all = gain_all[0:2] + gain_all[2:4] + gain_all[4:6]
        norm_all, ffn_all = gain_all[0], gain_all[1]

        mix_pieces = jnp.concatenate(
            [
                b_weight.reshape(FB, R, MW),
                c_weight.reshape(FB, R, MW),
                x_weight.reshape(FB, R, MW),
                out_weight.T.reshape(FB, R, MW),
            ],
            axis=2,
        ).transpose(1, 0, 2)
        mix_w = jnp.zeros((R, FB, 4 * MW), BF)
        for k in range(R):
            got = swap_row(pick(mix_pieces, r ^ k), k)
            mix_w = lax.dynamic_update_index_in_dim(mix_w, got, r ^ k, 0)
        mix_w = mix_w.reshape(D, 4 * MW)
        in_w = mix_w[:, : 3 * MW]
        out_t = mix_w[:, 3 * MW :]
        taps = lax.dynamic_slice(conv_weight, (0, r * MW), (3, MW))

        cot_parts = [
            swap_row(lax.dynamic_slice(cotangent, ((r ^ k) * TP, 0), (TP, FB)), k)
            for k in range(R)
        ]
        cot_parts = jnp.stack(cot_parts)
        cot_own = jnp.concatenate([pick(cot_parts, r ^ b) for b in range(R)], axis=-1)

        def group(piece):
            held = gather(piece, direct)
            return jnp.stack([held[n] for n in keys]).reshape(-1, D)

        def others(piece):
            far = jnp.stack([swap_dp(piece, k) for k in range(1, Z)])
            held = gather(far, staged)
            return jnp.stack([held[n] for n in keys]).reshape(-1, D)

        cot_group = group(cot_own)

        inputs = x_rows.astype(F32)
        inv_first = lax.rsqrt(jnp.mean(inputs * inputs, axis=1) + EPSILON)
        normed_one = (inputs * inv_first[:, None] * norm_all[None, :]).astype(BF)
        projected = dot_plain(normed_one, in_w)
        b_sum = projected[:, :MW]
        c_sum = projected[:, MW : 2 * MW]
        x_sum = projected[:, 2 * MW :]
        mixed_rows = b_sum * x_sum
        conv_out = causal_conv(mixed_rows, taps)
        gated_mix = (c_sum * conv_out).astype(BF)

        def token_pieces(values):
            values = values.reshape(C, R, TP, D)
            return {(kr, kc): pick(values[kc], r ^ kr) for kr, kc in keys}

        own_in = pick(x_rows.reshape(C, R, TP, D)[0], r).astype(F32)
        own_inv = pick(inv_first.reshape(C, R, TP)[0], r)
        hidden = own_in + scatter_sum(token_pieces(dot_against(gated_mix, out_t)), direct)
        inv_second = lax.rsqrt(jnp.mean(hidden * hidden, axis=1) + EPSILON)
        normed_two = (hidden * inv_second[:, None] * ffn_all[None, :]).astype(BF)
        two_group = group(normed_two)

        gu_w = jnp.zeros((R, FB, 2 * FW), BF)
        down_w = jnp.zeros((FW, D), BF)
        for k in range(R):
            to = r ^ k
            piece = jnp.concatenate(
                [
                    lax.dynamic_slice(gate_weight, (0, to * FW), (FB, FW)),
                    lax.dynamic_slice(up_weight, (0, to * FW), (FB, FW)),
                ],
                axis=1,
            )
            gu_w = lax.dynamic_update_index_in_dim(gu_w, swap_row(piece, k), to, 0)
            piece = lax.dynamic_slice(down_weight, (to * FW, 0), (FW, FB))
            down_w = lax.dynamic_update_slice(down_w, swap_row(piece, k), (0, to * FB))
        gu_w = gu_w.reshape(D, 2 * FW)

        def feed_forward(two, cot):
            sums = dot_plain(two, gu_w)
            gate_sum, up_sum = sums[:, :FW], sums[:, FW:]
            sigmoid_gate = jax.nn.sigmoid(gate_sum)
            activation = (gate_sum * sigmoid_gate * up_sum).astype(BF)
            act_delta = dot_against(cot, down_w)
            gate_delta = (
                act_delta * up_sum * sigmoid_gate * (1.0 + gate_sum * (1.0 - sigmoid_gate))
            ).astype(BF)
            up_delta = (act_delta * gate_sum * sigmoid_gate).astype(BF)
            return activation, jnp.concatenate([gate_delta, up_delta], axis=1)

        act_group, delta_group = feed_forward(two_group, cot_group)

        def split_pieces(values):
            values = values.reshape(len(keys), TP, D)
            return {n: values[i] for i, n in enumerate(keys)}

        two_delta = scatter_sum(split_pieces(dot_against(delta_group, gu_w)), direct)
        ffn_part = jnp.sum(two_delta * hidden * inv_second[:, None], axis=0)
        scaled = two_delta * ffn_all[None, :]
        average = jnp.mean(scaled * hidden, axis=1)
        hidden_delta = (
            cot_own.astype(F32)
            + inv_second[:, None] * scaled
            - hidden * (inv_second * inv_second * inv_second * average)[:, None]
        )
        mix_held = gather(hidden_delta.astype(BF), direct)
        mix_rel = jnp.stack([jnp.stack([mix_held[(kr, kc)] for kc in range(C)]) for kr in range(R)])
        mix_delta = jnp.stack([pick(mix_rel, r ^ b) for b in range(R)], axis=1).reshape(C * TB, D)

        gated_delta = dot_plain(mix_delta, out_t)
        c_delta = (gated_delta * conv_out).astype(BF)
        conv_delta = gated_delta * c_sum
        conv_part, mixed_delta = conv_backward(mixed_rows, conv_delta, taps)
        b_delta = (mixed_delta * x_sum).astype(BF)
        x_delta = (mixed_delta * b_sum).astype(BF)
        in_delta = jnp.concatenate([b_delta, c_delta, x_delta], axis=1)
        one_delta = scatter_sum(token_pieces(dot_against(in_delta, in_w)), direct)
        scaled = one_delta * norm_all[None, :]
        average = jnp.mean(scaled * own_in, axis=1)
        x_grad = (
            hidden_delta
            + own_inv[:, None] * scaled
            - own_in * (own_inv * own_inv * own_inv * average)[:, None]
        )

        def to_blocks(values):
            got = jnp.stack(
                [
                    swap_row(lax.dynamic_slice(values, (0, (r ^ k) * FB), (TP, FB)), k)
                    for k in range(R)
                ]
            )
            return jnp.concatenate([pick(got, r ^ b) for b in range(R)])

        x_grad = to_blocks(x_grad)
        block_own = hidden + scatter_sum(split_pieces(dot_plain(act_group, down_w)), direct)
        block_out = to_blocks(block_own)

        in_grad = dot_rows(normed_one, in_delta)
        norm_part = jnp.sum(in_grad * in_w.astype(F32), axis=1) / norm_all
        out_grad_t = dot_rows(mix_delta, gated_mix)
        QB = FB // Z
        body = jnp.concatenate([in_grad, out_grad_t], axis=1).reshape(R, Z, QB, 4 * MW)
        tail = jnp.zeros((R, EXTRA, max(4 * MW, FB)), F32)
        tail = tail.at[:, 0:3, :MW].set(conv_part[None])
        tail = tail.at[:, 3, :FB].set(norm_part.reshape(R, FB))
        tail = tail.at[:, 4, :FB].set(ffn_part.reshape(R, FB))
        wide_body = jnp.pad(body, ((0, 0), (0, 0), (0, 0), (0, tail.shape[2] - 4 * MW)))
        tail = jnp.broadcast_to(tail[:, None], (R, Z) + tail.shape[1:])
        packed = jnp.concatenate([wide_body, tail], axis=2)
        quarter = pick(packed, z, 1)
        for k in range(1, Z):
            quarter = quarter + swap_dp(pick(packed, z ^ k, 1).astype(BF), k).astype(F32)
        rows_got = jnp.stack([swap_row(pick(quarter, r ^ k).astype(BF), k) for k in range(R)])
        extra = rows_got[:, QB:].astype(F32)
        gain_sum = jnp.sum(extra[:, 3:5, :FB], axis=0)
        for kc in range(1, C):
            gain_sum = gain_sum + lax.ppermute(
                jnp.sum(extra[:, 3:5, :FB], axis=0), "col", [(i, i ^ kc) for i in range(C)]
            )
        conv_grad = jnp.concatenate([pick(extra[:, 0:3, :MW], r ^ b) for b in range(R)], axis=-1)
        mine = rows_got[:, :QB, : 4 * MW]
        by_z = jnp.stack([swap_dp(mine, k) for k in range(Z)])
        by_z = jnp.concatenate([pick(by_z, z ^ b) for b in range(Z)], axis=1)
        full = jnp.stack([pick(by_z, r ^ b) for b in range(R)], axis=1).astype(F32)
        b_grad = full[:, :, :MW].reshape(FB, R * MW)
        c_grad = full[:, :, MW : 2 * MW].reshape(FB, R * MW)
        x_weight_grad = full[:, :, 2 * MW : 3 * MW].reshape(FB, R * MW)
        out_grad = full[:, :, 3 * MW :].reshape(FB, R * MW).T

        cot_far = others(cot_own)
        two_far = others(normed_two)
        act_far, delta_far = feed_forward(two_far, cot_far)
        gu_grad = dot_rows(two_group, delta_group) + dot_rows(two_far, delta_far)
        dn_grad = dot_rows(act_group, cot_group) + dot_rows(act_far, cot_far)
        gu_got = jnp.stack(
            [
                swap_row(
                    lax.dynamic_slice(gu_grad, ((r ^ k) * FB, 0), (FB, 2 * FW)).astype(BF), k
                )
                for k in range(R)
            ]
        )
        gu_got = [pick(gu_got, r ^ b).astype(F32) for b in range(R)]
        gate_grad = jnp.concatenate([g[:, :FW] for g in gu_got], axis=1)
        up_grad = jnp.concatenate([g[:, FW:] for g in gu_got], axis=1)
        down_grad = jnp.zeros((R, FW, FB), F32)
        for k in range(R):
            to = r ^ k
            got = swap_row(lax.dynamic_slice(dn_grad, (0, to * FB), (FW, FB)).astype(BF), k)
            down_grad = lax.dynamic_update_index_in_dim(down_grad, got.astype(F32), to, 0)
        down_grad = down_grad.reshape(R * FW, FB)

        return (
            block_out,
            x_grad,
            gain_sum[0],
            b_grad,
            c_grad,
            x_weight_grad,
            conv_grad,
            out_grad,
            gain_sum[1],
            gate_grad,
            up_grad,
            down_grad,
        )

    placed = (
        P(("dp", "col"), "row"),
        P("row"),
        P("row", "col"),
        P("row", "col"),
        P("row", "col"),
        P(None, "col"),
        P("col", "row"),
        P("row"),
        P("row", "col"),
        P("row", "col"),
        P("col", "row"),
        P(("dp", "col"), "row"),
    )
    return jax.shard_map(
        local,
        mesh=mesh,
        in_specs=placed,
        out_specs=(
            P(("dp", "col"), "row"),
            P(("dp", "col"), "row"),
            P("row"),
            P("row", "col"),
            P("row", "col"),
            P("row", "col"),
            P(None, "col"),
            P("col", "row"),
            P("row"),
            P("row", "col"),
            P("row", "col"),
            P("col", "row"),
        ),
        check_vma=False,
    )
```

```python
import functools

import jax
import jax.numpy as jnp
from jax import lax
from jax.experimental import pallas as pl
from jax.experimental.pallas import tpu as pltpu
from jax.sharding import PartitionSpec as P


LEN = 128
EPSILON = 1e-05
BF = jnp.bfloat16
F32 = jnp.float32


def dot_rows(left_side, right_side):
    return lax.dot_general(
        left_side, right_side, (((0,), (0,)), ((), ())), preferred_element_type=F32
    )


def dot_against(left_side, right_side):
    return lax.dot_general(
        left_side, right_side, (((1,), (1,)), ((), ())), preferred_element_type=F32
    )


def dot_plain(left_side, right_side):
    return jnp.dot(left_side, right_side, preferred_element_type=F32)


def pick(values, index, axis=0):
    return lax.dynamic_index_in_dim(values, index, axis, keepdims=False)


def row_steps(rows):
    return 4 if rows % 64 == 0 else 1


def split_kernel(count, width, row_ref, left_ref, right_ref, *out_refs):
    for row in range(count):

        @pl.when(row_ref[0] == row)
        def _(row=row):
            for k, out_ref in enumerate(out_refs):
                at = (row ^ k) * width
                out_ref[:, :width] = left_ref[:, at : at + width]
                out_ref[:, width:] = right_ref[:, at : at + width]


def split_columns(row, count, left, right):
    rows, columns = left.shape
    width = columns // count
    step = rows // row_steps(rows)
    return pl.pallas_call(
        functools.partial(split_kernel, count, width),
        grid=(rows // step,),
        in_specs=[
            pl.BlockSpec(memory_space=pltpu.SMEM),
            pl.BlockSpec((step, columns), lambda i: (i, 0)),
            pl.BlockSpec((step, columns), lambda i: (i, 0)),
        ],
        out_specs=[pl.BlockSpec((step, 2 * width), lambda i: (i, 0))] * count,
        out_shape=[jax.ShapeDtypeStruct((rows, 2 * width), left.dtype)] * count,
        cost_estimate=pl.CostEstimate(
            flops=0, transcendentals=0, bytes_accessed=4 * 2 * rows * columns
        ),
    )(row.reshape(1), left, right)


def join_kernel(count, width, row_ref, *refs):
    parts, (left_ref, right_ref) = refs[:count], refs[count:]
    for row in range(count):

        @pl.when(row_ref[0] == row)
        def _(row=row):
            for k, part in enumerate(parts):
                at = (row ^ k) * width
                left_ref[:, at : at + width] = part[:, :width].astype(F32)
                right_ref[:, at : at + width] = part[:, width:].astype(F32)


def join_columns(row, parts):
    count = len(parts)
    rows, double = parts[0].shape
    width = double // 2
    step = rows // row_steps(rows)
    out_block = pl.BlockSpec((step, count * width), lambda i: (i, 0))
    out_shape = jax.ShapeDtypeStruct((rows, count * width), F32)
    return pl.pallas_call(
        functools.partial(join_kernel, count, width),
        grid=(rows // step,),
        in_specs=[pl.BlockSpec(memory_space=pltpu.SMEM)]
        + [pl.BlockSpec((step, double), lambda i: (i, 0))] * count,
        out_specs=[out_block] * 2,
        out_shape=[out_shape] * 2,
        cost_estimate=pl.CostEstimate(
            flops=0, transcendentals=0, bytes_accessed=6 * count * rows * double
        ),
    )(row.reshape(1), *parts)


def causal_conv(values, kernel):
    channels = values.shape[1]
    padded = jnp.pad(values.reshape(-1, LEN, channels), ((0, 0), (2, 0), (0, 0)))
    result = kernel[0] * padded[:, :-2] + kernel[1] * padded[:, 1:-1] + kernel[2] * padded[:, 2:]
    return result.reshape(values.shape)


def conv_backward(mixed_rows, conv_delta, kernel):
    channels = mixed_rows.shape[1]
    mixed_seqs = jnp.pad(mixed_rows.reshape(-1, LEN, channels), ((0, 0), (2, 0), (0, 0)))
    delta_seqs = conv_delta.reshape(-1, LEN, channels)
    kernel_grad = jnp.stack(
        [
            jnp.sum(delta_seqs * mixed_seqs[:, :-2], axis=(0, 1)),
            jnp.sum(delta_seqs * mixed_seqs[:, 1:-1], axis=(0, 1)),
            jnp.sum(delta_seqs * mixed_seqs[:, 2:], axis=(0, 1)),
        ]
    )
    delta_padded = jnp.pad(delta_seqs, ((0, 0), (0, 2), (0, 0)))
    mixed_delta = (
        kernel[0] * delta_padded[:, 2:]
        + kernel[1] * delta_padded[:, 1:-1]
        + kernel[2] * delta_padded[:, :-2]
    )
    return kernel_grad, mixed_delta.reshape(mixed_rows.shape)


def solution(mesh):
    Z, R, C = mesh.shape["dp"], mesh.shape["row"], mesh.shape["col"]

    def swap_row(values, k):
        if k == 0:
            return values
        return lax.ppermute(values, "row", [(i, i ^ k) for i in range(R)])

    def swap_dp(values, k):
        if k == 0:
            return values
        return lax.ppermute(values, "dp", [(i, i ^ k) for i in range(Z)])

    def swap_plane(values, key):
        kr, kc = key
        moves = [
            (i * C + j, (i ^ kr) * C + (j ^ kc)) for i in range(R) for j in range(C)
        ]
        return lax.ppermute(values, ("row", "col"), moves)

    high = [(kr, 0) for kr in range(2, R, 2)]
    wide = [(0, kc) for kc in range(1, C)]
    if (R // 2) * C <= 4:
        chip_stages = [[(kr, kc) for kr in range(0, R, 2) for kc in range(C)][1:]]
    else:
        chip_stages = [high, wide]
    highs = [(0, 0)] + high
    chips = [(kr, kc) for kc in range(C) for kr in range(0, R, 2)]

    def xor(a, b):
        return (a[0] ^ b[0], a[1] ^ b[1])

    def after(values, *others):
        return lax.optimization_barrier((values, others))[0]

    def exchange(held, stages):
        held = dict(held)
        for stage in stages:
            names = list(held)
            payload = held[names[0]]
            if len(names) > 1:
                payload = jnp.stack([held[n] for n in names])
            for offset in stage:
                got = swap_plane(payload, offset)
                for at, name in enumerate(names):
                    held[xor(name, offset)] = got[at] if len(names) > 1 else got
        return held

    def with_mates(held):
        payload = jnp.stack([held[n] for n in chips])
        got = swap_plane(payload, (1, 0))
        held = dict(held)
        for at, name in enumerate(chips):
            held[xor(name, (1, 0))] = got[at]
        return held

    def local(
        x_in,
        norm_gain,
        b_weight,
        c_weight,
        x_weight,
        conv_weight,
        out_weight,
        ffn_gain,
        gate_weight,
        up_weight,
        down_weight,
        cotangent,
    ):
        z = lax.axis_index("dp")
        r = lax.axis_index("row")
        TB, FB = x_in.shape
        D = FB * R
        TP = TB // R
        MW = b_weight.shape[1] // R
        FW = gate_weight.shape[1] // R

        def choose(values, index):
            if len(values) == 1:
                return values[0]
            if len(values) <= 4:
                middle = len(values) // 2
                return jnp.where(
                    index < middle,
                    choose(values[:middle], index),
                    choose(values[middle:], index - middle),
                )
            return pick(jnp.stack(values), index)

        def in_row_order(get):
            return [choose([get(b ^ i) for i in range(R)], r) for b in range(R)]

        def token_rows(held):
            rows = []
            for kc in range(C):
                rows = rows + in_row_order(lambda k: held[(k, kc)])
            return jnp.concatenate(rows, axis=-2)

        def column_rows(held):
            rows = []
            for kc in range(C):
                rows.append(jnp.concatenate(in_row_order(lambda k: held[(k, kc)]), axis=-1))
            return jnp.concatenate(rows, axis=-2)

        def block_rows(held):
            left, right = [], []
            for kc in range(C):
                row = in_row_order(lambda k: held[(k, kc)])
                left.append(jnp.concatenate([v[..., :FB] for v in row], axis=-1))
                right.append(jnp.concatenate([v[..., FB:] for v in row], axis=-1))
            return jnp.concatenate(left, axis=-2), jnp.concatenate(right, axis=-2)

        def scatter_sum(values):
            width = values.shape[1]
            values = values.reshape(C, R // 2, 2, TP, width)
            keep = choose([values[:, :, 0], values[:, :, 1]], r % 2)
            send = choose([values[:, :, 1], values[:, :, 0]], r % 2)
            chip = keep + swap_plane(send.astype(BF), (1, 0)).astype(F32)
            pieces = {}
            for kc in range(C):
                for h in range(R // 2):
                    order = [chip[kc, i ^ h] for i in range(R // 2)]
                    pieces[(2 * h, kc)] = choose(order, r // 2)
            return add_chips(pieces)

        def add_chips(pieces):
            for at in range(len(chip_stages) - 1, -1, -1):
                left = [(0, 0)]
                for stage in chip_stages[:at]:
                    left = left + [xor(n, o) for o in stage for n in left]
                total = {n: pieces[n] for n in left}
                for offset in chip_stages[at]:
                    payload = jnp.stack([pieces[xor(n, offset)].astype(BF) for n in left])
                    got = swap_plane(payload, offset)
                    for i, n in enumerate(left):
                        total[n] = total[n] + got[i].astype(F32)
                pieces = total
            return pieces[(0, 0)]

        def far_held(held):
            payload = jnp.stack([held[n] for n in highs])
            far = jnp.stack([swap_dp(payload, k) for k in range(1, Z)], axis=1)
            got = [far] + [swap_plane(far, offset) for offset in wide]
            out = {}
            for offset, part in zip([(0, 0)] + wide, got):
                for at, name in enumerate(highs):
                    out[xor(name, offset)] = part[at]
            return out

        gains = jnp.concatenate([norm_gain, ffn_gain])[None]
        part_a = lax.reduce_precision(gains, 8, 7)
        part_b = lax.reduce_precision(gains - part_a, 8, 7)
        part_c = gains - part_a - part_b
        gain_rows = jnp.concatenate([part_a, part_b, part_c]).astype(BF)
        gain_rows = jnp.pad(gain_rows, ((0, 13), (0, 0)))
        block = jnp.concatenate(
            [jnp.concatenate([x_in, cotangent], axis=1), gain_rows], axis=0
        )
        xc_held = exchange({(0, 0): block}, chip_stages)
        xc_all = with_mates(xc_held)
        x_group, cot_group = block_rows({n: v[:TB] for n, v in xc_all.items()})
        gain_got = in_row_order(lambda k: xc_all[(k, 0)][TB : TB + 3].astype(F32))
        gain_got = [jnp.sum(v, axis=0) for v in gain_got]
        norm_all = jnp.concatenate([v[:FB] for v in gain_got])
        ffn_all = jnp.concatenate([v[FB:] for v in gain_got])
        own_in = lax.dynamic_slice(x_group, (r * TP, 0), (TP, D)).astype(F32)
        cot_own = lax.dynamic_slice(cot_group, (r * TP, 0), (TP, D)).astype(F32)

        MP = max(3 * MW, FB)
        mix_got = []
        for k in range(R):
            at = (r ^ k) * MW
            piece = jnp.concatenate(
                [lax.dynamic_slice(w, (0, at), (FB, MW)) for w in (b_weight, c_weight, x_weight)],
                axis=1,
            )
            low = lax.dynamic_slice(out_weight, (at, 0), (MW, FB))
            piece = jnp.concatenate(
                [jnp.pad(piece, ((0, 0), (0, MP - 3 * MW))), jnp.pad(low, ((0, 0), (0, MP - FB)))]
            )
            mix_got.append(swap_row(piece, k))
        in_w = jnp.concatenate(in_row_order(lambda k: mix_got[k][:FB, : 3 * MW]), axis=0)
        out_w = jnp.concatenate(in_row_order(lambda k: mix_got[k][FB:, :FB]), axis=1)
        taps = lax.dynamic_slice(conv_weight, (0, r * MW), (3, MW))

        down_got = []
        gu_got = split_columns(r, R, gate_weight, up_weight)
        gu_got = [swap_row(piece, k) for k, piece in enumerate(gu_got)]
        for k in range(R):
            piece = lax.dynamic_slice(down_weight, ((r ^ k) * FW, 0), (FW, FB))
            down_got.append(swap_row(piece, k))
        gu_w = jnp.concatenate(in_row_order(lambda k: gu_got[k]), axis=0)
        down_w = jnp.concatenate(in_row_order(lambda k: down_got[k]), axis=1)
        gu_w, down_w = lax.optimization_barrier((gu_w, down_w))

        def mixer_forward(rows):
            inputs = rows.astype(F32)
            inverse = lax.rsqrt(jnp.mean(inputs * inputs, axis=1) + EPSILON)
            normed = (inputs * inverse[:, None] * norm_all[None, :]).astype(BF)
            sums = dot_plain(normed, in_w)
            b_sum, c_sum, x_sum = sums[:, :MW], sums[:, MW : 2 * MW], sums[:, 2 * MW :]
            mixed = b_sum * x_sum
            conv_out = causal_conv(mixed, taps)
            gated = (c_sum * conv_out).astype(BF)
            return normed, b_sum, c_sum, x_sum, mixed, conv_out, gated

        def mixer_backward(state, mix_delta):
            _, b_sum, c_sum, x_sum, mixed, conv_out, _ = state
            gated_delta = dot_against(mix_delta, out_w)
            c_delta = (gated_delta * conv_out).astype(BF)
            conv_part, mixed_delta = conv_backward(mixed, gated_delta * c_sum, taps)
            b_delta = (mixed_delta * x_sum).astype(BF)
            x_delta = (mixed_delta * b_sum).astype(BF)
            return jnp.concatenate([b_delta, c_delta, x_delta], axis=1), conv_part

        def feed_forward(two, cot):
            sums = dot_plain(two, gu_w)
            gate_sum, up_sum = sums[:, :FW], sums[:, FW:]
            sigmoid_gate = jax.nn.sigmoid(gate_sum)
            activation = (gate_sum * sigmoid_gate * up_sum).astype(BF)
            act_delta = dot_against(cot, down_w)
            gate_delta = (
                act_delta * up_sum * sigmoid_gate * (1.0 + gate_sum * (1.0 - sigmoid_gate))
            ).astype(BF)
            up_delta = (act_delta * gate_sum * sigmoid_gate).astype(BF)
            return activation, jnp.concatenate([gate_delta, up_delta], axis=1)

        state = mixer_forward(x_group)
        hidden_part = dot_plain(state[-1], out_w)
        hidden = own_in + scatter_sum(hidden_part)
        inv_second = lax.rsqrt(jnp.mean(hidden * hidden, axis=1) + EPSILON)
        normed_two = (hidden * inv_second[:, None] * ffn_all[None, :]).astype(BF)
        two_held = exchange({(0, 0): normed_two}, chip_stages)
        two_group = token_rows(with_mates(two_held))
        act_group, delta_group = feed_forward(two_group, cot_group)
        two_part = dot_against(delta_group, gu_w)
        two_delta = scatter_sum(two_part)
        scaled = two_delta * ffn_all[None, :]
        average = jnp.mean(scaled * hidden, axis=1)
        hidden_delta = (
            cot_own
            + inv_second[:, None] * scaled
            - hidden * (inv_second * inv_second * inv_second * average)[:, None]
        )
        mix_own = hidden_delta.astype(BF)
        mix_held = exchange({(0, 0): mix_own}, chip_stages)
        mix_group = token_rows(with_mates(mix_held))
        in_delta, conv_part = mixer_backward(state, mix_group)
        one_part = dot_against(in_delta, in_w)
        in_grad = dot_rows(state[0], in_delta)
        out_grad = dot_rows(state[-1], mix_group)
        norm_part = jnp.sum(in_grad * in_w.astype(F32), axis=1) / norm_all
        ffn_part = jnp.sum(two_delta * hidden * inv_second[:, None], axis=0)
        corner = MP - FB >= max(MW, FB // 2) and MW >= 8
        extras = jnp.zeros((R, 8, max(MW, FB // 2)), F32)
        extras = jnp.concatenate(
            [
                jnp.pad(
                    jnp.broadcast_to(conv_part[None], (R, 3, MW)),
                    ((0, 0), (0, 0), (0, max(MW, FB // 2) - MW)),
                ),
                jnp.pad(
                    jnp.concatenate(
                        [norm_part.reshape(R, 2, FB // 2), ffn_part.reshape(R, 2, FB // 2)],
                        axis=1,
                    ),
                    ((0, 0), (0, 0), (0, max(MW, FB // 2) - FB // 2)),
                ),
            ],
            axis=1,
        )
        low = out_grad.reshape(MW, R, FB).transpose(1, 0, 2)
        top = jnp.pad(in_grad.reshape(R, FB, 3 * MW), ((0, 0), (0, 0), (0, MP - 3 * MW)))
        if corner:
            room = ((0, 0), (0, MW - 7), (0, MP - FB - extras.shape[2]))
            low = jnp.concatenate([low, jnp.pad(extras, room)], axis=2)
            packed = jnp.concatenate([top, low], axis=1)
        else:
            low = jnp.pad(low, ((0, 0), (0, 0), (0, MP - FB)))
            rows = -(FB + MW + 7) % (16 * Z) + 7
            extras = jnp.pad(extras, ((0, 0), (0, rows - 7), (0, MP - extras.shape[2])))
            packed = jnp.concatenate([top, low, extras], axis=1)
        quarter_rows = packed.shape[1] // Z
        packed = packed.reshape(R, Z, quarter_rows, MP)
        quarter = pick(packed, z, 1)
        for k in range(1, Z):
            got = swap_dp(pick(packed, z ^ k, 1).astype(BF), k)
            quarter = quarter + got.astype(F32)
        quarter = quarter.astype(BF)
        mine = jnp.stack([swap_row(pick(quarter, r ^ k), k) for k in range(R)])
        by_z = [swap_dp(mine, k) for k in range(Z)]
        by_z = jnp.concatenate(
            [choose([by_z[b ^ i] for i in range(Z)], z) for b in range(Z)], axis=1
        )
        mix_back = [by_z[k] for k in range(R)]
        block_part = dot_plain(act_group, down_w)
        sums = scatter_sum(jnp.concatenate([one_part, block_part], axis=1))
        one_delta, block_own = sums[:, :D], sums[:, D:]
        inv_own = lax.rsqrt(jnp.mean(own_in * own_in, axis=1) + EPSILON)
        scaled = one_delta * norm_all[None, :]
        average = jnp.mean(scaled * own_in, axis=1)
        x_grad = (
            hidden_delta
            + inv_own[:, None] * scaled
            - own_in * (inv_own * inv_own * inv_own * average)[:, None]
        )
        ends = jnp.stack([hidden + block_own, x_grad])
        got = [
            swap_row(lax.dynamic_slice(ends, (0, 0, (r ^ k) * FB), (2, TP, FB)), k)
            for k in range(R)
        ]
        ends = jnp.concatenate(in_row_order(lambda k: got[k]), axis=1)

        cot_far = far_held({n: xc_held[n][:TB, FB:] for n in highs})
        two_far = far_held(two_held)
        cot_far = column_rows(with_mates(cot_far)).reshape(-1, D)
        two_far = token_rows(with_mates(two_far)).reshape(-1, D)
        two_far, cot_far = after((two_far, cot_far), in_delta)
        act_far, delta_far = feed_forward(two_far, cot_far)
        gu_grad = dot_rows(two_group, delta_group) + dot_rows(two_far, delta_far)
        dn_grad = dot_rows(act_group, cot_group) + dot_rows(act_far, cot_far)
        gu_back, dn_back = [], []
        for k in range(R):
            to = r ^ k
            piece = lax.dynamic_slice(dn_grad, (0, to * FB), (FW, FB)).astype(BF)
            dn_back.append(swap_row(piece, k))
            piece = lax.dynamic_slice(gu_grad, (to * FB, 0), (FB, 2 * FW)).astype(BF)
            gu_back.append(swap_row(piece, k))

        def joined(parts, cut, axis):
            return jnp.concatenate(
                in_row_order(lambda k: cut(parts[k]).astype(F32)), axis=axis
            )

        gate_grad, up_grad = join_columns(r, gu_back)
        down_grad = joined(dn_back, lambda g: g, 0)
        b_grad = joined(mix_back, lambda g: g[:FB, :MW], 1)
        c_grad = joined(mix_back, lambda g: g[:FB, MW : 2 * MW], 1)
        x_weight_grad = joined(mix_back, lambda g: g[:FB, 2 * MW : 3 * MW], 1)
        out_grad = joined(mix_back, lambda g: g[FB : FB + MW, :FB], 0)
        if corner:
            extras = [g[FB : FB + 7, FB:] for g in mix_back]
        else:
            extras = [g[FB + MW : FB + MW + 7] for g in mix_back]
        conv_grad = joined(extras, lambda g: g[0:3, :MW], 1)
        gain_part = sum(g[3:7, : FB // 2].astype(F32) for g in extras).reshape(2, FB)
        gain_sum = gain_part
        for kc in range(1, C):
            gain_sum = gain_sum + lax.ppermute(gain_part, "col", [(i, i ^ kc) for i in range(C)])

        return (
            ends[0],
            ends[1],
            gain_sum[0],
            b_grad,
            c_grad,
            x_weight_grad,
            conv_grad,
            out_grad,
            gain_sum[1],
            gate_grad,
            up_grad,
            down_grad,
        )

    placed = (
        P(("dp", "col"), "row"),
        P("row"),
        P("row", "col"),
        P("row", "col"),
        P("row", "col"),
        P(None, "col"),
        P("col", "row"),
        P("row"),
        P("row", "col"),
        P("row", "col"),
        P("col", "row"),
        P(("dp", "col"), "row"),
    )
    return jax.shard_map(
        local,
        mesh=mesh,
        in_specs=placed,
        out_specs=(
            P(("dp", "col"), "row"),
            P(("dp", "col"), "row"),
            P("row"),
            P("row", "col"),
            P("row", "col"),
            P("row", "col"),
            P(None, "col"),
            P("col", "row"),
            P("row"),
            P("row", "col"),
            P("row", "col"),
            P("col", "row"),
        ),
        check_vma=False,
    )
```

```python
import functools

import jax
import jax.numpy as jnp
from jax import lax
from jax.experimental import pallas as pl
from jax.experimental.pallas import tpu as pltpu
from jax.sharding import PartitionSpec as P


LEN = 128
EPSILON = 1e-05
BF = jnp.bfloat16
F32 = jnp.float32


def dot_rows(left_side, right_side):
    return lax.dot_general(
        left_side, right_side, (((0,), (0,)), ((), ())), preferred_element_type=F32
    )


def dot_against(left_side, right_side):
    return lax.dot_general(
        left_side, right_side, (((1,), (1,)), ((), ())), preferred_element_type=F32
    )


def dot_plain(left_side, right_side):
    return jnp.dot(left_side, right_side, preferred_element_type=F32)


def pick(values, index, axis=0):
    return lax.dynamic_index_in_dim(values, index, axis, keepdims=False)


def row_steps(rows):
    return 2 if rows % 32 == 0 else 1


def split_kernel(count, width, row_ref, left_ref, right_ref, *out_refs):
    for row in range(count):

        @pl.when(row_ref[0] == row)
        def _(row=row):
            for k, out_ref in enumerate(out_refs):
                at = (row ^ k) * width
                out_ref[:, :width] = left_ref[:, at : at + width]
                out_ref[:, width:] = right_ref[:, at : at + width]


def split_columns(row, count, left, right):
    rows, columns = left.shape
    width = columns // count
    step = rows // row_steps(rows)
    return pl.pallas_call(
        functools.partial(split_kernel, count, width),
        grid=(rows // step,),
        in_specs=[
            pl.BlockSpec(memory_space=pltpu.SMEM),
            pl.BlockSpec((step, columns), lambda i: (i, 0)),
            pl.BlockSpec((step, columns), lambda i: (i, 0)),
        ],
        out_specs=[pl.BlockSpec((step, 2 * width), lambda i: (i, 0))] * count,
        out_shape=[jax.ShapeDtypeStruct((rows, 2 * width), left.dtype)] * count,
        cost_estimate=pl.CostEstimate(
            flops=0, transcendentals=0, bytes_accessed=4 * 2 * rows * columns
        ),
    )(row.reshape(1), left, right)


def nbytes(*arrays):
    return sum(a.size * a.dtype.itemsize for a in arrays)


def whole_call(kernel, row, arrays, shapes):
    out = pl.pallas_call(
        kernel,
        in_specs=[pl.BlockSpec(memory_space=pltpu.SMEM)]
        + [pl.BlockSpec(memory_space=pltpu.VMEM)] * len(arrays),
        out_specs=[pl.BlockSpec(memory_space=pltpu.VMEM)] * len(shapes),
        out_shape=shapes,
        cost_estimate=pl.CostEstimate(
            flops=0, transcendentals=0, bytes_accessed=nbytes(*arrays) + nbytes(*shapes)
        ),
    )(row.reshape(1), *arrays)
    return out


def first_kernel(chips, size, row_ref, own_ref, mate_ref, x_ref, cot_ref, one_ref, gain_ref):
    width = own_ref.shape[-1] // 2
    for at, (kr, kc) in enumerate(chips):
        for core, ref in ((0, own_ref), (1, mate_ref)):
            slot = row_ref[0] ^ (kr ^ core)
            where = pl.ds(pl.multiple_of(slot * width, width), width)
            x_ref[kc * size : (kc + 1) * size, where] = ref[at, 0:size, :width]
            cot_ref[kc * size : (kc + 1) * size, where] = ref[at, 0:size, width:]
            if kc == 0:
                parts = ref[at, size : size + 16, :].astype(F32)
                both = parts[0:1] + parts[1:2] + parts[2:3]
                gain_ref[0:1, where] = both[:, :width]
                gain_ref[1:2, where] = both[:, width:]
    rows, features = x_ref.shape
    step = min(64, rows)
    for start in range(0, rows, step):
        values = x_ref[start : start + step, :].astype(F32)
        total = jnp.sum(values * values, axis=1, keepdims=True)
        inverse = lax.rsqrt(total / features + EPSILON)
        one_ref[start : start + step, :] = (values * inverse * gain_ref[0:1, :]).astype(BF)


def join_kernel(count, width, row_ref, *refs):
    parts, (left_ref, right_ref) = refs[:count], refs[count:]
    for row in range(count):

        @pl.when(row_ref[0] == row)
        def _(row=row):
            for k, part in enumerate(parts):
                at = (row ^ k) * width
                left_ref[:, at : at + width] = part[:, :width].astype(F32)
                right_ref[:, at : at + width] = part[:, width:].astype(F32)


def join_columns(row, parts):
    count = len(parts)
    rows, double = parts[0].shape
    width = double // 2
    step = rows // row_steps(rows)
    out_block = pl.BlockSpec((step, count * width), lambda i: (i, 0))
    out_shape = jax.ShapeDtypeStruct((rows, count * width), F32)
    return pl.pallas_call(
        functools.partial(join_kernel, count, width),
        grid=(rows // step,),
        in_specs=[pl.BlockSpec(memory_space=pltpu.SMEM)]
        + [pl.BlockSpec((step, double), lambda i: (i, 0))] * count,
        out_specs=[out_block] * 2,
        out_shape=[out_shape] * 2,
        cost_estimate=pl.CostEstimate(
            flops=0, transcendentals=0, bytes_accessed=6 * count * rows * double
        ),
    )(row.reshape(1), *parts)


def mix_join_kernel(sizes, row_ref, z_ref, *refs):
    groups, count, deep, wide, _, spare_row, spare_lane = sizes
    parts = refs[:groups]
    b_ref, c_ref, x_ref, out_ref, conv_ref, gain_ref, held = refs[groups:]
    quarter = parts[0].shape[1]
    for i, part in enumerate(parts):
        start = pl.multiple_of((z_ref[0] ^ i) * quarter, quarter)
        held[:, pl.ds(start, quarter), :] = part[...]
    half = deep // 2
    gain = jnp.zeros((8, half), F32)
    for k in range(count):
        spare = held[k, spare_row : spare_row + 16, spare_lane : spare_lane + half]
        gain = gain + spare.astype(F32)[:8]
    gain_ref[...] = gain
    for row in range(count):

        @pl.when(row_ref[0] == row)
        def _(row=row):
            for k in range(count):
                at = (row ^ k) * wide
                for n, ref in enumerate((b_ref, c_ref, x_ref)):
                    block = held[k, :deep, n * wide : (n + 1) * wide]
                    ref[:, at : at + wide] = block.astype(F32)
                out_ref[at : at + wide, :] = held[k, deep : deep + wide, :deep].astype(F32)
                spare = held[k, spare_row : spare_row + 16, spare_lane : spare_lane + wide]
                conv_ref[:, at : at + wide] = spare.astype(F32)[:8]


def mix_join(row, z, parts, count, deep, wide, spare_row, spare_lane):
    groups = len(parts)
    quarter, lanes = parts[0].shape[1:]
    sizes = (groups, count, deep, wide, lanes, spare_row, spare_lane)
    shapes = [jax.ShapeDtypeStruct((deep, count * wide), F32)] * 3 + [
        jax.ShapeDtypeStruct((count * wide, deep), F32),
        jax.ShapeDtypeStruct((8, count * wide), F32),
        jax.ShapeDtypeStruct((8, deep // 2), F32),
    ]
    return pl.pallas_call(
        functools.partial(mix_join_kernel, sizes),
        in_specs=[pl.BlockSpec(memory_space=pltpu.SMEM)] * 2
        + [pl.BlockSpec(memory_space=pltpu.VMEM)] * groups,
        out_specs=[pl.BlockSpec(memory_space=pltpu.VMEM)] * 6,
        out_shape=shapes,
        scratch_shapes=[pltpu.VMEM((count, groups * quarter, lanes), BF)],
        cost_estimate=pl.CostEstimate(
            flops=0, transcendentals=0, bytes_accessed=nbytes(*parts) + nbytes(*shapes)
        ),
    )(row.reshape(1), z.reshape(1), *parts)


def causal_conv(values, kernel):
    channels = values.shape[1]
    padded = jnp.pad(values.reshape(-1, LEN, channels), ((0, 0), (2, 0), (0, 0)))
    result = kernel[0] * padded[:, :-2] + kernel[1] * padded[:, 1:-1] + kernel[2] * padded[:, 2:]
    return result.reshape(values.shape)


def conv_backward(mixed_rows, conv_delta, kernel):
    channels = mixed_rows.shape[1]
    mixed_seqs = jnp.pad(mixed_rows.reshape(-1, LEN, channels), ((0, 0), (2, 0), (0, 0)))
    delta_seqs = conv_delta.reshape(-1, LEN, channels)
    kernel_grad = jnp.stack(
        [
            jnp.sum(delta_seqs * mixed_seqs[:, :-2], axis=(0, 1)),
            jnp.sum(delta_seqs * mixed_seqs[:, 1:-1], axis=(0, 1)),
            jnp.sum(delta_seqs * mixed_seqs[:, 2:], axis=(0, 1)),
        ]
    )
    delta_padded = jnp.pad(delta_seqs, ((0, 0), (0, 2), (0, 0)))
    mixed_delta = (
        kernel[0] * delta_padded[:, 2:]
        + kernel[1] * delta_padded[:, 1:-1]
        + kernel[2] * delta_padded[:, :-2]
    )
    return kernel_grad, mixed_delta.reshape(mixed_rows.shape)


def solution(mesh):
    Z, R, C = mesh.shape["dp"], mesh.shape["row"], mesh.shape["col"]

    def swap_row(values, k):
        if k == 0:
            return values
        return lax.ppermute(values, "row", [(i, i ^ k) for i in range(R)])

    def swap_dp(values, k):
        if k == 0:
            return values
        return lax.ppermute(values, "dp", [(i, i ^ k) for i in range(Z)])

    def swap_plane(values, key):
        kr, kc = key
        moves = [
            (i * C + j, (i ^ kr) * C + (j ^ kc)) for i in range(R) for j in range(C)
        ]
        return lax.ppermute(values, ("row", "col"), moves)

    high = [(kr, 0) for kr in range(2, R, 2)]
    wide = [(0, kc) for kc in range(1, C)]
    if (R // 2) * C <= 4:
        chip_stages = [[(kr, kc) for kr in range(0, R, 2) for kc in range(C)][1:]]
    else:
        chip_stages = [high, wide]
    highs = [(0, 0)] + high
    chips = [(kr, kc) for kc in range(C) for kr in range(0, R, 2)]

    def xor(a, b):
        return (a[0] ^ b[0], a[1] ^ b[1])

    def after(values, *others):
        return lax.optimization_barrier((values, others))[0]

    def exchange(held, stages):
        held = dict(held)
        for stage in stages:
            names = list(held)
            payload = held[names[0]]
            if len(names) > 1:
                payload = jnp.stack([held[n] for n in names])
            for offset in stage:
                got = swap_plane(payload, offset)
                for at, name in enumerate(names):
                    held[xor(name, offset)] = got[at] if len(names) > 1 else got
        return held

    def with_mates(held, *gates):
        payload = jnp.stack([held[n] for n in chips])
        if gates:
            payload = after(payload, *gates)
        got = swap_plane(payload, (1, 0))
        held = dict(held)
        for at, name in enumerate(chips):
            held[xor(name, (1, 0))] = got[at]
        return held

    def local(
        x_in,
        norm_gain,
        b_weight,
        c_weight,
        x_weight,
        conv_weight,
        out_weight,
        ffn_gain,
        gate_weight,
        up_weight,
        down_weight,
        cotangent,
    ):
        z = lax.axis_index("dp")
        r = lax.axis_index("row")
        TB, FB = x_in.shape
        D = FB * R
        TP = TB // R
        MW = b_weight.shape[1] // R
        FW = gate_weight.shape[1] // R

        def choose(values, index):
            if len(values) == 1:
                return values[0]
            if len(values) <= 4:
                middle = len(values) // 2
                return jnp.where(
                    index < middle,
                    choose(values[:middle], index),
                    choose(values[middle:], index - middle),
                )
            return pick(jnp.stack(values), index)

        def in_row_order(get):
            return [choose([get(b ^ i) for i in range(R)], r) for b in range(R)]

        def token_rows(held):
            rows = []
            for kc in range(C):
                rows = rows + in_row_order(lambda k: held[(k, kc)])
            return jnp.concatenate(rows, axis=-2)

        def column_rows(held):
            rows = []
            for kc in range(C):
                rows.append(jnp.concatenate(in_row_order(lambda k: held[(k, kc)]), axis=-1))
            return jnp.concatenate(rows, axis=-2)

        def scatter_sum(values):
            width = values.shape[1]
            values = values.reshape(C, R // 2, 2, TP, width)
            keep = choose([values[:, :, 0], values[:, :, 1]], r % 2)
            send = choose([values[:, :, 1], values[:, :, 0]], r % 2)
            chip = keep + swap_plane(send.astype(BF), (1, 0)).astype(F32)
            pieces = {}
            for kc in range(C):
                for h in range(R // 2):
                    order = [chip[kc, i ^ h] for i in range(R // 2)]
                    pieces[(2 * h, kc)] = choose(order, r // 2)
            return add_chips(pieces)

        def add_chips(pieces):
            for at in range(len(chip_stages) - 1, -1, -1):
                left = [(0, 0)]
                for stage in chip_stages[:at]:
                    left = left + [xor(n, o) for o in stage for n in left]
                total = {n: pieces[n] for n in left}
                for offset in chip_stages[at]:
                    payload = jnp.stack([pieces[xor(n, offset)].astype(BF) for n in left])
                    got = swap_plane(payload, offset)
                    for i, n in enumerate(left):
                        total[n] = total[n] + got[i].astype(F32)
                pieces = total
            return pieces[(0, 0)]

        def grow(groups, offsets):
            names = [n for some, _ in groups for n in some]
            arrays = [array for _, array in groups]
            payload = jnp.concatenate(arrays) if len(arrays) > 1 else arrays[0]
            return [(names, payload)] + [
                ([xor(n, offset) for n in names], swap_plane(payload, offset))
                for offset in offsets
            ]

        def far_pieces(groups, *gates):
            groups = [(names, after(array, *gates)) for names, array in groups]
            mates = [
                ([xor(n, (1, 0)) for n in names], swap_plane(array, (1, 0)))
                for names, array in groups
            ]
            return {
                n: array[at] for names, array in groups + mates for at, n in enumerate(names)
            }

        gains = jnp.concatenate([norm_gain, ffn_gain])[None]
        part_a = lax.reduce_precision(gains, 8, 7)
        part_b = lax.reduce_precision(gains - part_a, 8, 7)
        part_c = gains - part_a - part_b
        gain_rows = jnp.concatenate([part_a, part_b, part_c]).astype(BF)
        gain_rows = jnp.pad(gain_rows, ((0, 13), (0, 0)))
        block = jnp.concatenate(
            [jnp.concatenate([x_in, cotangent], axis=1), gain_rows], axis=0
        )
        xc_held = exchange({(0, 0): block}, chip_stages)
        xc_own = jnp.stack([xc_held[n] for n in chips])
        xc_all = (xc_own, swap_plane(xc_own, (1, 0)))
        x_group, cot_group, normed_one, gain_all = whole_call(
            functools.partial(first_kernel, chips, TB),
            r,
            xc_all,
            [jax.ShapeDtypeStruct((C * TB, D), BF)] * 3 + [jax.ShapeDtypeStruct((8, D), F32)],
        )
        norm_all, ffn_all = gain_all[0], gain_all[1]
        own_in = lax.dynamic_slice(x_group, (r * TP, 0), (TP, D)).astype(F32)
        cot_own = lax.dynamic_slice(cot_group, (r * TP, 0), (TP, D)).astype(F32)

        MP = max(3 * MW, FB)
        mix_got = []
        for k in range(R):
            at = (r ^ k) * MW
            piece = jnp.concatenate(
                [lax.dynamic_slice(w, (0, at), (FB, MW)) for w in (b_weight, c_weight, x_weight)],
                axis=1,
            )
            low = lax.dynamic_slice(out_weight, (at, 0), (MW, FB))
            piece = jnp.concatenate(
                [jnp.pad(piece, ((0, 0), (0, MP - 3 * MW))), jnp.pad(low, ((0, 0), (0, MP - FB)))]
            )
            mix_got.append(swap_row(piece, k))
        taps = lax.dynamic_slice(conv_weight, (0, r * MW), (3, MW))
        in_w = jnp.concatenate(in_row_order(lambda k: mix_got[k][:FB, : 3 * MW]), axis=0)
        out_w = jnp.concatenate(in_row_order(lambda k: mix_got[k][FB:, :FB]), axis=1)

        down_got = []
        gu_got = split_columns(r, R, gate_weight, up_weight)
        gu_got = [swap_row(piece, k) for k, piece in enumerate(gu_got)]
        for k in range(R):
            piece = lax.dynamic_slice(down_weight, ((r ^ k) * FW, 0), (FW, FB))
            down_got.append(swap_row(piece, k))
        gu_w = jnp.concatenate(in_row_order(lambda k: gu_got[k]), axis=0)
        gu_w = lax.optimization_barrier(gu_w)
        down_w = jnp.concatenate(in_row_order(lambda k: down_got[k]), axis=1)
        down_w = lax.optimization_barrier(down_w)

        def mixer_forward(normed):
            sums = dot_plain(normed, in_w)
            b_sum, c_sum, x_sum = sums[:, :MW], sums[:, MW : 2 * MW], sums[:, 2 * MW :]
            mixed = b_sum * x_sum
            conv_out = causal_conv(mixed, taps)
            gated = (c_sum * conv_out).astype(BF)
            return normed, b_sum, c_sum, x_sum, mixed, conv_out, gated

        def mixer_backward(state, mix_delta):
            _, b_sum, c_sum, x_sum, mixed, conv_out, _ = state
            gated_delta = dot_against(mix_delta, out_w)
            c_delta = (gated_delta * conv_out).astype(BF)
            conv_part, mixed_delta = conv_backward(mixed, gated_delta * c_sum, taps)
            b_delta = (mixed_delta * x_sum).astype(BF)
            x_delta = (mixed_delta * b_sum).astype(BF)
            return jnp.concatenate([b_delta, c_delta, x_delta], axis=1), conv_part

        def feed_forward(two, cot):
            sums = dot_plain(two, gu_w)
            gate_sum, up_sum = sums[:, :FW], sums[:, FW:]
            sigmoid_gate = jax.nn.sigmoid(gate_sum)
            activation = (gate_sum * sigmoid_gate * up_sum).astype(BF)
            act_delta = dot_against(cot, down_w)
            gate_delta = (
                act_delta * up_sum * sigmoid_gate * (1.0 + gate_sum * (1.0 - sigmoid_gate))
            ).astype(BF)
            up_delta = (act_delta * gate_sum * sigmoid_gate).astype(BF)
            return activation, jnp.concatenate([gate_delta, up_delta], axis=1)

        state = mixer_forward(normed_one)
        hidden_part = dot_plain(state[-1], out_w)
        hidden = own_in + scatter_sum(hidden_part)
        inv_second = lax.rsqrt(jnp.mean(hidden * hidden, axis=1) + EPSILON)
        normed_two = (hidden * inv_second[:, None] * ffn_all[None, :]).astype(BF)
        two_held = exchange({(0, 0): normed_two}, chip_stages)
        two_group = token_rows(with_mates(two_held))
        act_group, delta_group = feed_forward(two_group, cot_group)
        two_part = dot_against(delta_group, gu_w)
        two_delta = scatter_sum(two_part)
        scaled = two_delta * ffn_all[None, :]
        average = jnp.mean(scaled * hidden, axis=1)
        hidden_delta = (
            cot_own
            + inv_second[:, None] * scaled
            - hidden * (inv_second * inv_second * inv_second * average)[:, None]
        )
        mix_own = hidden_delta.astype(BF)
        mix_held = exchange({(0, 0): mix_own}, chip_stages)
        mix_group = lax.optimization_barrier(token_rows(with_mates(mix_held)))
        in_delta, conv_part = mixer_backward(state, mix_group)
        one_part = dot_against(in_delta, in_w)
        in_grad = dot_rows(state[0], in_delta)
        out_grad = dot_rows(state[-1], mix_group)
        norm_part = jnp.sum(in_grad * in_w.astype(F32), axis=1) / norm_all
        ffn_part = jnp.sum(two_delta * hidden * inv_second[:, None], axis=0)
        corner = MP - FB >= max(MW, FB // 2) and MW >= 8
        extras = jnp.zeros((R, 8, max(MW, FB // 2)), F32)
        extras = jnp.concatenate(
            [
                jnp.pad(
                    jnp.broadcast_to(conv_part[None], (R, 3, MW)),
                    ((0, 0), (0, 0), (0, max(MW, FB // 2) - MW)),
                ),
                jnp.pad(
                    jnp.concatenate(
                        [norm_part.reshape(R, 2, FB // 2), ffn_part.reshape(R, 2, FB // 2)],
                        axis=1,
                    ),
                    ((0, 0), (0, 0), (0, max(MW, FB // 2) - FB // 2)),
                ),
            ],
            axis=1,
        )
        low = out_grad.reshape(MW, R, FB).transpose(1, 0, 2)
        top = jnp.pad(in_grad.reshape(R, FB, 3 * MW), ((0, 0), (0, 0), (0, MP - 3 * MW)))
        if corner:
            room = ((0, 0), (0, MW - 7), (0, MP - FB - extras.shape[2]))
            low = jnp.concatenate([low, jnp.pad(extras, room)], axis=2)
            packed = jnp.concatenate([top, low], axis=1)
        else:
            low = jnp.pad(low, ((0, 0), (0, 0), (0, MP - FB)))
            rows = -(FB + MW + 7) % (16 * Z) + 7
            extras = jnp.pad(extras, ((0, 0), (0, rows - 7), (0, MP - extras.shape[2])))
            packed = jnp.concatenate([top, low, extras], axis=1)
        quarter_rows = packed.shape[1] // Z
        packed = packed.reshape(R, Z, quarter_rows, MP)
        quarter = pick(packed, z, 1)
        for k in range(1, Z):
            got = swap_dp(pick(packed, z ^ k, 1).astype(BF), k)
            quarter = quarter + got.astype(F32)
        quarter = quarter.astype(BF)
        mine = jnp.stack([swap_row(pick(quarter, r ^ k), k) for k in range(R)])
        by_z = [swap_dp(mine, k) for k in range(Z)]
        block_part = dot_plain(after(act_group, packed), down_w)
        sums = scatter_sum(jnp.concatenate([one_part, block_part], axis=1))
        one_delta, block_own = sums[:, :D], sums[:, D:]
        inv_own = lax.rsqrt(jnp.mean(own_in * own_in, axis=1) + EPSILON)
        scaled = one_delta * norm_all[None, :]
        average = jnp.mean(scaled * own_in, axis=1)
        x_grad = (
            hidden_delta
            + inv_own[:, None] * scaled
            - own_in * (inv_own * inv_own * inv_own * average)[:, None]
        )
        ends = jnp.stack([hidden + block_own, x_grad])
        got = [
            swap_row(lax.dynamic_slice(ends, (0, 0, (r ^ k) * FB), (2, TP, FB)), k)
            for k in range(R)
        ]
        ends = jnp.concatenate(in_row_order(lambda k: got[k]), axis=1)

        payload = jnp.stack([xc_held[n][:TB, FB:] for n in highs])
        far = jnp.stack([swap_dp(payload, k) for k in range(1, Z)], axis=1)
        cot_groups = grow([(highs, far)], wide)
        far = jnp.stack([swap_dp(normed_two, k) for k in range(1, Z)])[None]
        two_groups = grow([([(0, 0)], far)], high)
        two_groups = grow(two_groups, wide)
        cot_far = column_rows(far_pieces(cot_groups, packed)).reshape(-1, D)
        two_far = token_rows(far_pieces(two_groups, packed)).reshape(-1, D)
        two_far, cot_far = after((two_far, cot_far), in_delta)
        act_far, delta_far = feed_forward(two_far, cot_far)
        dn_grad = dot_rows(act_group, cot_group) + dot_rows(act_far, cot_far)
        gu_grad = dot_rows(two_group, delta_group) + dot_rows(two_far, delta_far)
        gu_back, dn_back = [], []
        for k in range(R):
            to = r ^ k
            piece = lax.dynamic_slice(dn_grad, (0, to * FB), (FW, FB)).astype(BF)
            dn_back.append(swap_row(piece, k))
            piece = lax.dynamic_slice(gu_grad, (to * FB, 0), (FB, 2 * FW)).astype(BF)
            gu_back.append(swap_row(piece, k))

        def joined(parts, cut, axis):
            return jnp.concatenate(
                in_row_order(lambda k: cut(parts[k]).astype(F32)), axis=axis
            )

        gate_grad, up_grad = join_columns(r, gu_back)
        down_grad = joined(dn_back, lambda g: g, 0)
        spare = (FB, FB) if corner else (FB + MW, 0)
        b_grad, c_grad, x_weight_grad, out_grad, conv_grad, gain_rows = mix_join(
            r, z, by_z, R, FB, MW, *spare
        )
        conv_grad = conv_grad[:3]
        gain_part = gain_rows[3:7].reshape(2, FB)
        gain_sum = gain_part
        for kc in range(1, C):
            gain_sum = gain_sum + lax.ppermute(gain_part, "col", [(i, i ^ kc) for i in range(C)])

        return (
            ends[0],
            ends[1],
            gain_sum[0],
            b_grad,
            c_grad,
            x_weight_grad,
            conv_grad,
            out_grad,
            gain_sum[1],
            gate_grad,
            up_grad,
            down_grad,
        )

    placed = (
        P(("dp", "col"), "row"),
        P("row"),
        P("row", "col"),
        P("row", "col"),
        P("row", "col"),
        P(None, "col"),
        P("col", "row"),
        P("row"),
        P("row", "col"),
        P("row", "col"),
        P("col", "row"),
        P(("dp", "col"), "row"),
    )
    return jax.shard_map(
        local,
        mesh=mesh,
        in_specs=placed,
        out_specs=(
            P(("dp", "col"), "row"),
            P(("dp", "col"), "row"),
            P("row"),
            P("row", "col"),
            P("row", "col"),
            P("row", "col"),
            P(None, "col"),
            P("col", "row"),
            P("row"),
            P("row", "col"),
            P("row", "col"),
            P("col", "row"),
        ),
        check_vma=False,
    )
```

```python
import functools

import jax
import jax.numpy as jnp
from jax import lax
from jax.experimental import pallas as pl
from jax.experimental.pallas import tpu as pltpu
from jax.sharding import PartitionSpec as P


LEN = 128
EPSILON = 1e-05
BF = jnp.bfloat16
F32 = jnp.float32


def dot_rows(left_side, right_side):
    return lax.dot_general(
        left_side, right_side, (((0,), (0,)), ((), ())), preferred_element_type=F32
    )


def dot_against(left_side, right_side):
    return lax.dot_general(
        left_side, right_side, (((1,), (1,)), ((), ())), preferred_element_type=F32
    )


def dot_plain(left_side, right_side):
    return jnp.dot(left_side, right_side, preferred_element_type=F32)


def pick(values, index, axis=0):
    return lax.dynamic_index_in_dim(values, index, axis, keepdims=False)


def row_steps(rows):
    return 2 if rows % 32 == 0 else 1


def by_chunks(rows, body, step=16):
    step = step if rows % step == 0 else rows

    def run(i, carry):
        body(pl.ds(pl.multiple_of(i * step, step), step))
        return carry

    if step == rows:
        body(slice(0, rows))
    else:
        lax.fori_loop(0, rows // step, run, 0)


def split_kernel(count, width, row_ref, left_ref, right_ref, *out_refs):
    for row in range(count):

        @pl.when(row_ref[0] == row)
        def _(row=row):
            def body(where):
                for k, out_ref in enumerate(out_refs):
                    at = (row ^ k) * width
                    out_ref[where, :width] = left_ref[where, at : at + width]
                    out_ref[where, width:] = right_ref[where, at : at + width]

            by_chunks(left_ref.shape[0], body)


def split_columns(row, count, left, right):
    rows, columns = left.shape
    width = columns // count
    step = rows // row_steps(rows)
    return pl.pallas_call(
        functools.partial(split_kernel, count, width),
        grid=(rows // step,),
        in_specs=[
            pl.BlockSpec(memory_space=pltpu.SMEM),
            pl.BlockSpec((step, columns), lambda i: (i, 0)),
            pl.BlockSpec((step, columns), lambda i: (i, 0)),
        ],
        out_specs=[pl.BlockSpec((step, 2 * width), lambda i: (i, 0))] * count,
        out_shape=[jax.ShapeDtypeStruct((rows, 2 * width), left.dtype)] * count,
        cost_estimate=pl.CostEstimate(
            flops=0, transcendentals=0, bytes_accessed=4 * 2 * rows * columns
        ),
    )(row.reshape(1), left, right)


def ffn_kernel(width, two_ref, cot_ref, gu_ref, down_ref, act_ref, delta_ref):
    sums = dot_plain(two_ref[...], gu_ref[...])
    act_delta = dot_against(cot_ref[...], down_ref[...])
    gate_sum, up_sum = sums[:, :width], sums[:, width:]
    sigmoid_gate = jax.nn.sigmoid(gate_sum)
    silu = gate_sum * sigmoid_gate
    act_ref[...] = (silu * up_sum).astype(BF)
    slope = sigmoid_gate * (1.0 + gate_sum * (1.0 - sigmoid_gate))
    delta_ref[:, :width] = (act_delta * up_sum * slope).astype(BF)
    delta_ref[:, width:] = (act_delta * silu).astype(BF)


def ffn_call(two, cot, gu_w, down_w):
    rows, features = two.shape
    width = down_w.shape[0]
    tile = 256 if rows % 256 == 0 else rows
    tokens = pl.BlockSpec((tile, features), lambda i: (i, 0))
    return pl.pallas_call(
        functools.partial(ffn_kernel, width),
        grid=(rows // tile,),
        in_specs=[
            tokens,
            tokens,
            pl.BlockSpec(gu_w.shape, lambda i: (0, 0)),
            pl.BlockSpec(down_w.shape, lambda i: (0, 0)),
        ],
        out_specs=[
            pl.BlockSpec((tile, width), lambda i: (i, 0)),
            pl.BlockSpec((tile, 2 * width), lambda i: (i, 0)),
        ],
        out_shape=[
            jax.ShapeDtypeStruct((rows, width), BF),
            jax.ShapeDtypeStruct((rows, 2 * width), BF),
        ],
        cost_estimate=pl.CostEstimate(
            flops=6 * rows * features * width,
            transcendentals=rows * width,
            bytes_accessed=2 * (2 * rows * features + 3 * features * width + 3 * rows * width),
        ),
    )(two, cot, gu_w, down_w)


def nbytes(*arrays):
    return sum(a.size * a.dtype.itemsize for a in arrays)


def whole_call(kernel, row, arrays, shapes):
    out = pl.pallas_call(
        kernel,
        in_specs=[pl.BlockSpec(memory_space=pltpu.SMEM)]
        + [pl.BlockSpec(memory_space=pltpu.VMEM)] * len(arrays),
        out_specs=[pl.BlockSpec(memory_space=pltpu.VMEM)] * len(shapes),
        out_shape=shapes,
        cost_estimate=pl.CostEstimate(
            flops=0, transcendentals=0, bytes_accessed=nbytes(*arrays) + nbytes(*shapes)
        ),
    )(row.reshape(1), *arrays)
    return out


def first_kernel(chips, size, row_ref, own_ref, mate_ref, x_ref, cot_ref, one_ref, gain_ref):
    width = own_ref.shape[-1] // 2
    for at, (kr, kc) in enumerate(chips):
        for core, ref in ((0, own_ref), (1, mate_ref)):
            slot = row_ref[0] ^ (kr ^ core)
            where = pl.ds(pl.multiple_of(slot * width, width), width)
            x_ref[kc * size : (kc + 1) * size, where] = ref[at, 0:size, :width]
            cot_ref[kc * size : (kc + 1) * size, where] = ref[at, 0:size, width:]
            if kc == 0:
                parts = ref[at, size : size + 16, :].astype(F32)
                both = parts[0:1] + parts[1:2] + parts[2:3]
                gain_ref[0:1, where] = both[:, :width]
                gain_ref[1:2, where] = both[:, width:]
    rows, features = x_ref.shape

    def normalize(where):
        values = x_ref[where, :].astype(F32)
        total = jnp.sum(values * values, axis=1, keepdims=True)
        inverse = lax.rsqrt(total / features + EPSILON)
        one_ref[where, :] = (values * inverse * gain_ref[0:1, :]).astype(BF)

    by_chunks(rows, normalize, 64)


def join_kernel(count, width, row_ref, *refs):
    parts, (left_ref, right_ref) = refs[:count], refs[count:]
    for row in range(count):

        @pl.when(row_ref[0] == row)
        def _(row=row):
            def body(where):
                for k, part in enumerate(parts):
                    at = (row ^ k) * width
                    left_ref[where, at : at + width] = part[where, :width].astype(F32)
                    right_ref[where, at : at + width] = part[where, width:].astype(F32)

            by_chunks(left_ref.shape[0], body)


def join_columns(row, parts):
    count = len(parts)
    rows, double = parts[0].shape
    width = double // 2
    step = rows // row_steps(rows)
    out_block = pl.BlockSpec((step, count * width), lambda i: (i, 0))
    out_shape = jax.ShapeDtypeStruct((rows, count * width), F32)
    return pl.pallas_call(
        functools.partial(join_kernel, count, width),
        grid=(rows // step,),
        in_specs=[pl.BlockSpec(memory_space=pltpu.SMEM)]
        + [pl.BlockSpec((step, double), lambda i: (i, 0))] * count,
        out_specs=[out_block] * 2,
        out_shape=[out_shape] * 2,
        cost_estimate=pl.CostEstimate(
            flops=0, transcendentals=0, bytes_accessed=6 * count * rows * double
        ),
    )(row.reshape(1), *parts)


def mix_join_kernel(sizes, row_ref, z_ref, *refs):
    groups, count, deep, wide, _, spare_row, spare_lane = sizes
    parts = refs[:groups]
    b_ref, c_ref, x_ref, out_ref, conv_ref, gain_ref, held = refs[groups:]
    quarter = parts[0].shape[1]
    for i, part in enumerate(parts):
        start = pl.multiple_of((z_ref[0] ^ i) * quarter, quarter)
        held[:, pl.ds(start, quarter), :] = part[...]
    half = deep // 2
    gain = jnp.zeros((8, half), F32)
    for k in range(count):
        spare = held[k, spare_row : spare_row + 16, spare_lane : spare_lane + half]
        gain = gain + spare.astype(F32)[:8]
    gain_ref[...] = gain
    for row in range(count):

        @pl.when(row_ref[0] == row)
        def _(row=row):
            for k in range(count):
                at = (row ^ k) * wide

                def body(where, k=k, at=at):
                    for n, ref in enumerate((b_ref, c_ref, x_ref)):
                        block = held[k, where, n * wide : (n + 1) * wide]
                        ref[where, at : at + wide] = block.astype(F32)

                by_chunks(deep, body)
                out_ref[at : at + wide, :] = held[k, deep : deep + wide, :deep].astype(F32)
                spare = held[k, spare_row : spare_row + 16, spare_lane : spare_lane + wide]
                conv_ref[:, at : at + wide] = spare.astype(F32)[:8]


def mix_join(row, z, parts, count, deep, wide, spare_row, spare_lane):
    groups = len(parts)
    quarter, lanes = parts[0].shape[1:]
    sizes = (groups, count, deep, wide, lanes, spare_row, spare_lane)
    shapes = [jax.ShapeDtypeStruct((deep, count * wide), F32)] * 3 + [
        jax.ShapeDtypeStruct((count * wide, deep), F32),
        jax.ShapeDtypeStruct((8, count * wide), F32),
        jax.ShapeDtypeStruct((8, deep // 2), F32),
    ]
    return pl.pallas_call(
        functools.partial(mix_join_kernel, sizes),
        in_specs=[pl.BlockSpec(memory_space=pltpu.SMEM)] * 2
        + [pl.BlockSpec(memory_space=pltpu.VMEM)] * groups,
        out_specs=[pl.BlockSpec(memory_space=pltpu.VMEM)] * 6,
        out_shape=shapes,
        scratch_shapes=[pltpu.VMEM((count, groups * quarter, lanes), BF)],
        cost_estimate=pl.CostEstimate(
            flops=0, transcendentals=0, bytes_accessed=nbytes(*parts) + nbytes(*shapes)
        ),
    )(row.reshape(1), z.reshape(1), *parts)


def causal_conv(values, kernel):
    channels = values.shape[1]
    padded = jnp.pad(values.reshape(-1, LEN, channels), ((0, 0), (2, 0), (0, 0)))
    result = kernel[0] * padded[:, :-2] + kernel[1] * padded[:, 1:-1] + kernel[2] * padded[:, 2:]
    return result.reshape(values.shape)


def conv_backward(mixed_rows, conv_delta, kernel):
    channels = mixed_rows.shape[1]
    mixed_seqs = jnp.pad(mixed_rows.reshape(-1, LEN, channels), ((0, 0), (2, 0), (0, 0)))
    delta_seqs = conv_delta.reshape(-1, LEN, channels)
    kernel_grad = jnp.stack(
        [
            jnp.sum(delta_seqs * mixed_seqs[:, :-2], axis=(0, 1)),
            jnp.sum(delta_seqs * mixed_seqs[:, 1:-1], axis=(0, 1)),
            jnp.sum(delta_seqs * mixed_seqs[:, 2:], axis=(0, 1)),
        ]
    )
    delta_padded = jnp.pad(delta_seqs, ((0, 0), (0, 2), (0, 0)))
    mixed_delta = (
        kernel[0] * delta_padded[:, 2:]
        + kernel[1] * delta_padded[:, 1:-1]
        + kernel[2] * delta_padded[:, :-2]
    )
    return kernel_grad, mixed_delta.reshape(mixed_rows.shape)


def solution(mesh):
    Z, R, C = mesh.shape["dp"], mesh.shape["row"], mesh.shape["col"]

    def swap_row(values, k):
        if k == 0:
            return values
        return lax.ppermute(values, "row", [(i, i ^ k) for i in range(R)])

    def swap_dp(values, k):
        if k == 0:
            return values
        return lax.ppermute(values, "dp", [(i, i ^ k) for i in range(Z)])

    def swap_plane(values, key):
        kr, kc = key
        moves = [
            (i * C + j, (i ^ kr) * C + (j ^ kc)) for i in range(R) for j in range(C)
        ]
        return lax.ppermute(values, ("row", "col"), moves)

    high = [(kr, 0) for kr in range(2, R, 2)]
    wide = [(0, kc) for kc in range(1, C)]
    if (R // 2) * C <= 4:
        chip_stages = [[(kr, kc) for kr in range(0, R, 2) for kc in range(C)][1:]]
    else:
        chip_stages = [high, wide]
    highs = [(0, 0)] + high
    chips = [(kr, kc) for kc in range(C) for kr in range(0, R, 2)]

    def xor(a, b):
        return (a[0] ^ b[0], a[1] ^ b[1])

    def after(values, *others):
        return lax.optimization_barrier((values, others))[0]

    def exchange(held, stages):
        held = dict(held)
        for stage in stages:
            names = list(held)
            payload = held[names[0]]
            if len(names) > 1:
                payload = jnp.stack([held[n] for n in names])
            for offset in stage:
                got = swap_plane(payload, offset)
                for at, name in enumerate(names):
                    held[xor(name, offset)] = got[at] if len(names) > 1 else got
        return held

    def with_mates(held, *gates):
        payload = jnp.stack([held[n] for n in chips])
        if gates:
            payload = after(payload, *gates)
        got = swap_plane(payload, (1, 0))
        held = dict(held)
        for at, name in enumerate(chips):
            held[xor(name, (1, 0))] = got[at]
        return held

    def local(
        x_in,
        norm_gain,
        b_weight,
        c_weight,
        x_weight,
        conv_weight,
        out_weight,
        ffn_gain,
        gate_weight,
        up_weight,
        down_weight,
        cotangent,
    ):
        z = lax.axis_index("dp")
        r = lax.axis_index("row")
        TB, FB = x_in.shape
        D = FB * R
        TP = TB // R
        MW = b_weight.shape[1] // R
        FW = gate_weight.shape[1] // R

        def choose(values, index):
            if len(values) == 1:
                return values[0]
            if len(values) <= 4:
                middle = len(values) // 2
                return jnp.where(
                    index < middle,
                    choose(values[:middle], index),
                    choose(values[middle:], index - middle),
                )
            return pick(jnp.stack(values), index)

        def in_row_order(get):
            return [choose([get(b ^ i) for i in range(R)], r) for b in range(R)]

        def token_rows(held):
            rows = []
            for kc in range(C):
                rows = rows + in_row_order(lambda k: held[(k, kc)])
            return jnp.concatenate(rows, axis=-2)

        def column_rows(held):
            rows = []
            for kc in range(C):
                rows.append(jnp.concatenate(in_row_order(lambda k: held[(k, kc)]), axis=-1))
            return jnp.concatenate(rows, axis=-2)

        def scatter_sum(values):
            width = values.shape[1]
            values = values.reshape(C, R // 2, 2, TP, width)
            keep = choose([values[:, :, 0], values[:, :, 1]], r % 2)
            send = choose([values[:, :, 1], values[:, :, 0]], r % 2)
            chip = keep + swap_plane(send.astype(BF), (1, 0)).astype(F32)
            pieces = {}
            for kc in range(C):
                for h in range(R // 2):
                    order = [chip[kc, i ^ h] for i in range(R // 2)]
                    pieces[(2 * h, kc)] = choose(order, r // 2)
            return add_chips(pieces)

        def add_chips(pieces):
            for at in range(len(chip_stages) - 1, -1, -1):
                left = [(0, 0)]
                for stage in chip_stages[:at]:
                    left = left + [xor(n, o) for o in stage for n in left]
                total = {n: pieces[n] for n in left}
                for offset in chip_stages[at]:
                    payload = jnp.stack([pieces[xor(n, offset)].astype(BF) for n in left])
                    got = swap_plane(payload, offset)
                    for i, n in enumerate(left):
                        total[n] = total[n] + got[i].astype(F32)
                pieces = total
            return pieces[(0, 0)]

        def grow(groups, offsets):
            names = [n for some, _ in groups for n in some]
            arrays = [array for _, array in groups]
            payload = jnp.concatenate(arrays) if len(arrays) > 1 else arrays[0]
            return [(names, payload)] + [
                ([xor(n, offset) for n in names], swap_plane(payload, offset))
                for offset in offsets
            ]

        def far_pieces(groups, *gates):
            groups = [(names, after(array, *gates)) for names, array in groups]
            mates = [
                ([xor(n, (1, 0)) for n in names], swap_plane(array, (1, 0)))
                for names, array in groups
            ]
            return {
                n: array[at] for names, array in groups + mates for at, n in enumerate(names)
            }

        gains = jnp.concatenate([norm_gain, ffn_gain])[None]
        part_a = lax.reduce_precision(gains, 8, 7)
        part_b = lax.reduce_precision(gains - part_a, 8, 7)
        part_c = gains - part_a - part_b
        gain_rows = jnp.concatenate([part_a, part_b, part_c]).astype(BF)
        gain_rows = jnp.pad(gain_rows, ((0, 13), (0, 0)))
        block = jnp.concatenate(
            [jnp.concatenate([x_in, cotangent], axis=1), gain_rows], axis=0
        )
        xc_held = exchange({(0, 0): block}, chip_stages)
        xc_own = jnp.stack([xc_held[n] for n in chips])
        xc_all = (xc_own, swap_plane(xc_own, (1, 0)))
        x_group, cot_group, normed_one, gain_all = whole_call(
            functools.partial(first_kernel, chips, TB),
            r,
            xc_all,
            [jax.ShapeDtypeStruct((C * TB, D), BF)] * 3 + [jax.ShapeDtypeStruct((8, D), F32)],
        )
        norm_all, ffn_all = gain_all[0], gain_all[1]
        own_in = lax.dynamic_slice(x_group, (r * TP, 0), (TP, D)).astype(F32)
        cot_own = lax.dynamic_slice(cot_group, (r * TP, 0), (TP, D)).astype(F32)

        MP = max(3 * MW, FB)
        mix_got = []
        for k in range(R):
            at = (r ^ k) * MW
            piece = jnp.concatenate(
                [lax.dynamic_slice(w, (0, at), (FB, MW)) for w in (b_weight, c_weight, x_weight)],
                axis=1,
            )
            low = lax.dynamic_slice(out_weight, (at, 0), (MW, FB))
            piece = jnp.concatenate(
                [jnp.pad(piece, ((0, 0), (0, MP - 3 * MW))), jnp.pad(low, ((0, 0), (0, MP - FB)))]
            )
            mix_got.append(swap_row(piece, k))
        taps = lax.dynamic_slice(conv_weight, (0, r * MW), (3, MW))
        in_w = jnp.concatenate(in_row_order(lambda k: mix_got[k][:FB, : 3 * MW]), axis=0)
        out_w = jnp.concatenate(in_row_order(lambda k: mix_got[k][FB:, :FB]), axis=1)

        down_got = []
        gu_got = split_columns(r, R, gate_weight, up_weight)
        gu_got = [swap_row(piece, k) for k, piece in enumerate(gu_got)]
        for k in range(R):
            piece = lax.dynamic_slice(down_weight, ((r ^ k) * FW, 0), (FW, FB))
            down_got.append(swap_row(piece, k))
        gu_w = jnp.concatenate(in_row_order(lambda k: gu_got[k]), axis=0)
        gu_w = lax.optimization_barrier(gu_w)
        down_w = jnp.concatenate(in_row_order(lambda k: down_got[k]), axis=1)
        down_w = lax.optimization_barrier(down_w)

        def mixer_forward(normed):
            sums = dot_plain(normed, in_w)
            b_sum, c_sum, x_sum = sums[:, :MW], sums[:, MW : 2 * MW], sums[:, 2 * MW :]
            mixed = b_sum * x_sum
            conv_out = causal_conv(mixed, taps)
            gated = (c_sum * conv_out).astype(BF)
            return normed, b_sum, c_sum, x_sum, mixed, conv_out, gated

        def mixer_backward(state, mix_delta):
            _, b_sum, c_sum, x_sum, mixed, conv_out, _ = state
            gated_delta = dot_against(mix_delta, out_w)
            c_delta = (gated_delta * conv_out).astype(BF)
            conv_part, mixed_delta = conv_backward(mixed, gated_delta * c_sum, taps)
            b_delta = (mixed_delta * x_sum).astype(BF)
            x_delta = (mixed_delta * b_sum).astype(BF)
            return jnp.concatenate([b_delta, c_delta, x_delta], axis=1), conv_part

        def feed_forward(two, cot):
            sums = dot_plain(two, gu_w)
            gate_sum, up_sum = sums[:, :FW], sums[:, FW:]
            sigmoid_gate = jax.nn.sigmoid(gate_sum)
            activation = (gate_sum * sigmoid_gate * up_sum).astype(BF)
            act_delta = dot_against(cot, down_w)
            gate_delta = (
                act_delta * up_sum * sigmoid_gate * (1.0 + gate_sum * (1.0 - sigmoid_gate))
            ).astype(BF)
            up_delta = (act_delta * gate_sum * sigmoid_gate).astype(BF)
            return activation, jnp.concatenate([gate_delta, up_delta], axis=1)

        state = mixer_forward(normed_one)
        hidden_part = dot_plain(state[-1], out_w)
        hidden = own_in + scatter_sum(hidden_part)
        inv_second = lax.rsqrt(jnp.mean(hidden * hidden, axis=1) + EPSILON)
        normed_two = (hidden * inv_second[:, None] * ffn_all[None, :]).astype(BF)
        two_held = exchange({(0, 0): normed_two}, chip_stages)
        two_group = token_rows(with_mates(two_held))
        act_group, delta_group = feed_forward(two_group, cot_group)
        two_part = dot_against(delta_group, gu_w)
        two_delta = scatter_sum(two_part)
        scaled = two_delta * ffn_all[None, :]
        average = jnp.mean(scaled * hidden, axis=1)
        hidden_delta = (
            cot_own
            + inv_second[:, None] * scaled
            - hidden * (inv_second * inv_second * inv_second * average)[:, None]
        )
        mix_own = hidden_delta.astype(BF)
        mix_held = exchange({(0, 0): mix_own}, chip_stages)
        mix_group = lax.optimization_barrier(token_rows(with_mates(mix_held)))
        in_delta, conv_part = mixer_backward(state, mix_group)
        one_part = dot_against(in_delta, in_w)
        in_grad = dot_rows(state[0], in_delta)
        out_grad = dot_rows(state[-1], mix_group)
        norm_part = jnp.sum(in_grad * in_w.astype(F32), axis=1) / norm_all
        ffn_part = jnp.sum(two_delta * hidden * inv_second[:, None], axis=0)
        corner = MP - FB >= max(MW, FB // 2) and MW >= 8
        extras = jnp.zeros((R, 8, max(MW, FB // 2)), F32)
        extras = jnp.concatenate(
            [
                jnp.pad(
                    jnp.broadcast_to(conv_part[None], (R, 3, MW)),
                    ((0, 0), (0, 0), (0, max(MW, FB // 2) - MW)),
                ),
                jnp.pad(
                    jnp.concatenate(
                        [norm_part.reshape(R, 2, FB // 2), ffn_part.reshape(R, 2, FB // 2)],
                        axis=1,
                    ),
                    ((0, 0), (0, 0), (0, max(MW, FB // 2) - FB // 2)),
                ),
            ],
            axis=1,
        )
        low = out_grad.reshape(MW, R, FB).transpose(1, 0, 2)
        top = jnp.pad(in_grad.reshape(R, FB, 3 * MW), ((0, 0), (0, 0), (0, MP - 3 * MW)))
        if corner:
            room = ((0, 0), (0, MW - 7), (0, MP - FB - extras.shape[2]))
            low = jnp.concatenate([low, jnp.pad(extras, room)], axis=2)
            packed = jnp.concatenate([top, low], axis=1)
        else:
            low = jnp.pad(low, ((0, 0), (0, 0), (0, MP - FB)))
            rows = -(FB + MW + 7) % (16 * Z) + 7
            extras = jnp.pad(extras, ((0, 0), (0, rows - 7), (0, MP - extras.shape[2])))
            packed = jnp.concatenate([top, low, extras], axis=1)
        quarter_rows = packed.shape[1] // Z
        packed = packed.reshape(R, Z, quarter_rows, MP)
        quarter = pick(packed, z, 1)
        for k in range(1, Z):
            got = swap_dp(pick(packed, z ^ k, 1).astype(BF), k)
            quarter = quarter + got.astype(F32)
        quarter = quarter.astype(BF)
        mine = jnp.stack([swap_row(pick(quarter, r ^ k), k) for k in range(R)])
        by_z = [swap_dp(mine, k) for k in range(Z)]
        block_part = dot_plain(after(act_group, packed), down_w)
        sums = scatter_sum(jnp.concatenate([one_part, block_part], axis=1))
        one_delta, block_own = sums[:, :D], sums[:, D:]
        inv_own = lax.rsqrt(jnp.mean(own_in * own_in, axis=1) + EPSILON)
        scaled = one_delta * norm_all[None, :]
        average = jnp.mean(scaled * own_in, axis=1)
        x_grad = (
            hidden_delta
            + inv_own[:, None] * scaled
            - own_in * (inv_own * inv_own * inv_own * average)[:, None]
        )
        ends = jnp.stack([hidden + block_own, x_grad])
        got = [
            swap_row(lax.dynamic_slice(ends, (0, 0, (r ^ k) * FB), (2, TP, FB)), k)
            for k in range(R)
        ]
        ends = jnp.concatenate(in_row_order(lambda k: got[k]), axis=1)

        payload = jnp.stack([xc_held[n][:TB, FB:] for n in highs])
        far = jnp.stack([swap_dp(payload, k) for k in range(1, Z)], axis=1)
        cot_groups = grow([(highs, far)], wide)
        far = jnp.stack([swap_dp(normed_two, k) for k in range(1, Z)])[None]
        two_groups = grow([([(0, 0)], far)], high)
        two_groups = grow(two_groups, wide)
        cot_far = column_rows(far_pieces(cot_groups, packed)).reshape(-1, D)
        two_far = token_rows(far_pieces(two_groups, packed)).reshape(-1, D)
        two_far, cot_far = after((two_far, cot_far), in_delta)
        act_far, delta_far = ffn_call(two_far, cot_far, gu_w, down_w)
        dn_grad = dot_rows(act_group, cot_group) + dot_rows(act_far, cot_far)
        gu_grad = dot_rows(two_group, delta_group) + dot_rows(two_far, delta_far)
        gu_back, dn_back = [], []
        for k in range(R):
            to = r ^ k
            piece = lax.dynamic_slice(dn_grad, (0, to * FB), (FW, FB)).astype(BF)
            dn_back.append(swap_row(piece, k))
            piece = lax.dynamic_slice(gu_grad, (to * FB, 0), (FB, 2 * FW)).astype(BF)
            gu_back.append(swap_row(piece, k))

        def joined(parts, cut, axis):
            return jnp.concatenate(
                in_row_order(lambda k: cut(parts[k]).astype(F32)), axis=axis
            )

        gate_grad, up_grad = join_columns(r, gu_back)
        down_grad = joined(dn_back, lambda g: g, 0)
        spare = (FB, FB) if corner else (FB + MW, 0)
        b_grad, c_grad, x_weight_grad, out_grad, conv_grad, gain_rows = mix_join(
            r, z, by_z, R, FB, MW, *spare
        )
        conv_grad = conv_grad[:3]
        gain_part = gain_rows[3:7].reshape(2, FB)
        gain_sum = gain_part
        for kc in range(1, C):
            gain_sum = gain_sum + lax.ppermute(gain_part, "col", [(i, i ^ kc) for i in range(C)])

        return (
            ends[0],
            ends[1],
            gain_sum[0],
            b_grad,
            c_grad,
            x_weight_grad,
            conv_grad,
            out_grad,
            gain_sum[1],
            gate_grad,
            up_grad,
            down_grad,
        )

    placed = (
        P(("dp", "col"), "row"),
        P("row"),
        P("row", "col"),
        P("row", "col"),
        P("row", "col"),
        P(None, "col"),
        P("col", "row"),
        P("row"),
        P("row", "col"),
        P("row", "col"),
        P("col", "row"),
        P(("dp", "col"), "row"),
    )
    return jax.shard_map(
        local,
        mesh=mesh,
        in_specs=placed,
        out_specs=(
            P(("dp", "col"), "row"),
            P(("dp", "col"), "row"),
            P("row"),
            P("row", "col"),
            P("row", "col"),
            P("row", "col"),
            P(None, "col"),
            P("col", "row"),
            P("row"),
            P("row", "col"),
            P("row", "col"),
            P("col", "row"),
        ),
        check_vma=False,
    )
```
